32 devices in a mesh: group: 2 (over x), dev: 8 (over z, y), head: 2 (over core).
Axes of the slice: x: 2, y: 2, z: 4, core: 2. Of those that a mesh axis runs over, the one named last changes fastest.
Arguments:
- residual_in: bfloat16 [2048, 4096], P(('group', 'dev')), parts along dimension 0, may hold values from -6 to 6
- queries: bfloat16 [2048, 48, 128], P(('group', 'dev'), 'head'), parts along dimension 0, may hold values from -400 to 400
- key_cache: bfloat16 [32, 2048, 4, 128], P(('group', 'dev'), None, 'head'), parts along dimension 0, may hold values from -6 to 6
- value_cache: bfloat16 [32, 2048, 4, 128], P(('group', 'dev'), None, 'head'), parts along dimension 0, may hold values from -6 to 6
- new_keys: bfloat16 [2048, 4, 128], P(('group', 'dev'), 'head'), parts along dimension 0, may hold values from -6 to 6
- new_values: bfloat16 [2048, 4, 128], P(('group', 'dev'), 'head'), parts along dimension 0, may hold values from -6 to 6
- prefix_len: int32 [32], P(('group', 'dev')), parts along dimension 0, may hold values from 512 to 2048
- o_weight: bfloat16 [6144, 4096], P('head', 'dev'), may hold values from -0.078125 to 0.078125
- norm_gain: float32 [4096], replicated, may hold values from 0.5 to 1.5
- expert_ids: int32 [2048, 8], P(('group', 'dev')), parts along dimension 0, may hold values from 0 to 15, all different within a row; in each aligned block of 128 rows (0 to 127, 128 to 255, ...) at most 80 rows name the same one
- route_weights: float32 [2048, 8], P(('group', 'dev')), parts along dimension 0, may hold values from 0.1 to 0.4
- capacity: int32 [32], P('group'), parts along dimension 0, may hold values from 256 to 640
- gate_w: bfloat16 [16, 4096, 1408], P('dev', None, 'head'), may hold values from -0.09375 to 0.09375
- up_w: bfloat16 [16, 4096, 1408], P('dev', None, 'head'), may hold values from -0.09375 to 0.09375
- down_w: bfloat16 [16, 1408, 4096], P('dev', 'head'), may hold values from -0.15625 to 0.15625
Outputs:
- hidden: bfloat16 [2048, 4096], P(('group', 'dev'), 'head'), parts along dimension 0
- moe_out: bfloat16 [2048, 4096], P(('group', 'dev'), 'head'), parts along dimension 0
The draws below stay inside these ranges and needn't reach their ends.
There are 2 independent parts, one for each index of `group`. The reference program is written for one: setup_inputs(seed, part) draws one part's arguments, and reference() takes and returns one part's arrays. A program takes and returns all parts, laid end to end along the dimension named above; an argument that names none is the same for every part. Nothing has to cross between parts.
Inputs may be any that keep to these rules, and one draw needn't show every extreme that they name: `expert_ids`: each row names 8 different experts; among the tokens of one index of dev no expert is named more than 80 times.
All inputs are finite; a program needn't handle non-finite values.
Results may differ from the reference program's by a relative error of at most 0.014.
Values may be sent and summed in bfloat16 or wider, within the bound.
No kernel may reach another device: no remote copies, remote signals or barrier semaphores. Data moves between devices by JAX's collectives and lax.ppermute only.
A program may use at most 128 MiB of HBM per device.

```python
import math
import jax
import jax.numpy as jnp
import numpy as np
from jax import lax

D = 4096
QH = 48
KVH = 4
HD = 128
FF = 1408
EXPERTS = 16
TOP = 8
RESP = 64
PREFIX = 2048
TOK_DEV = 128
TOKENS = 1024
SEQS = 16
CAP = 80
N_DEV = 8
N_HEAD = 2


def attention_pair(key):
    base_keys = jax.random.truncated_normal(jax.random.fold_in(key, 101), -6.0, 6.0, (SEQS, PREFIX, KVH, HD), jnp.float32)
    base_queries = jax.random.truncated_normal(jax.random.fold_in(key, 102), -6.0, 6.0, (TOKENS, QH, HD), jnp.float32)
    return (base_queries, base_keys)


def draw_queries(key, part):
    return attention_pair(key)[0].astype(jnp.bfloat16)


def draw_key_cache(key, part):
    return attention_pair(key)[1].astype(jnp.bfloat16)


def draw_prefix_len(key, part):
    lowest = PREFIX // 4
    lengths = jax.random.randint(jax.random.fold_in(key, 201), (SEQS,), lowest, PREFIX + 1)
    picked = jax.random.randint(jax.random.fold_in(key, 202), (), 0, SEQS)
    lengths = lengths.at[picked].set(PREFIX).at[(picked + 1) % SEQS].set(lowest)
    return lengths.astype(jnp.int32)


def draw_capacity(key, part):
    lowest = TOKENS * TOP // EXPERTS // 2
    highest = TOKENS // TOK_DEV * CAP
    limits = jax.random.randint(jax.random.fold_in(key, 301), (EXPERTS,), lowest, highest + 1)
    picked = jax.random.randint(jax.random.fold_in(key, 302), (), 0, EXPERTS)
    limits = limits.at[picked].set(highest).at[(picked + 1) % EXPERTS].set(lowest)
    return limits.astype(jnp.int32)


def block_scale(key, extent, cuts, smallest, top_value):
    gain = 1.0
    for dim, shards_of in cuts:
        draws = jax.random.uniform(jax.random.fold_in(jax.random.fold_in(key, 6), dim), (shards_of,), jnp.float32, smallest / len(cuts), top_value / len(cuts))
        gain = gain * jnp.repeat(jnp.exp(draws), extent[dim] // shards_of).reshape((-1,) + (1,) * (len(extent) - 1 - dim))
    return gain


def routed_block(own_key, own, number, rows, count, top, reach, lean):
    ranking = jax.random.permutation(own_key, count)
    packed, common = portions_of(count, rows * top, reach, lean, True), portions_of(count, rows * top, reach, lean, False)
    places = jnp.arange(count)

    def named(sizes, offset_by):
        used = int((sizes > 0).sum())
        fixed = max(1, used // 4)
        moved = fixed + (places - fixed + offset_by * (used - fixed)) % max(1, count - fixed)
        return jnp.zeros((count,), jnp.int32).at[ranking[jnp.where(places < fixed, places, moved)]].set(jnp.asarray(sizes, jnp.int32))

    sizes = jnp.where(number % 4 == 0, named(packed, number // 4), named(common, number - number // 4 - 1))
    mixed = jax.random.permutation(jax.random.fold_in(own, 3), count)
    donor, sink = mixed[0:count // 2 * 2:2], mixed[1:count // 2 * 2:2]
    room = jnp.minimum(sizes[donor] - 1, reach - sizes[sink]) // 2
    room = jnp.where((donor == ranking[0]) | (sink == ranking[0]) | (sizes[sink] == 0), 0, jnp.maximum(room, 0))
    moved = jax.random.randint(jax.random.fold_in(own, 4), (count // 2,), 0, 1 << 20) % (room + 1)
    sizes = sizes.at[donor].add(-moved).at[sink].add(moved)
    labels = jnp.searchsorted(jnp.cumsum(sizes), jnp.arange(rows * top), side="right").astype(jnp.int32)
    table = labels.reshape(top, rows).T
    table = table[jax.random.permutation(jax.random.fold_in(own, 1), rows)]
    offset_by = jax.random.randint(jax.random.fold_in(own, 2), (rows, 1), 0, top)
    return jnp.take_along_axis(table, (jnp.arange(top)[None, :] + offset_by) % top, axis=1)


def portions_of(number_of, total, bound, lean, full):
    portions = [(1 << 20) // math.isqrt(standing ** lean) + 1 for standing in range(1, number_of + 1)]
    largest = bound if full else min(bound, max(-(-total // number_of), total * portions[0] // sum(portions)))
    least = 1 if total - largest >= number_of - 1 else 0
    given, spare = [largest] + [least] * (number_of - 1), total - largest - least * (number_of - 1)
    while spare > 0:
        movable = [i for i in range(1, number_of) if given[i] < largest] or [i for i in range(1, number_of) if given[i] < bound]
        mass, budget = sum([portions[i] for i in movable]), spare
        for i in movable:
            addition = min(bound - given[i], max(1, budget * portions[i] // mass), spare)
            given[i] = given[i] + addition
            spare = spare - addition
    return np.array(given)


def gaussian(key, shape, spread, reach, cuts=(), kind=jnp.bfloat16):
    drawn = jax.random.normal(key, shape, jnp.float32) * spread
    if len(cuts) > 0:
        drawn = block_scale(key, shape, cuts, -0.22, 0.18) * drawn
    return jnp.clip(drawn, min=-reach, max=reach).astype(kind)


def setup_inputs(seed: int = 0, part: int = 0) -> dict:
    keys = jax.random.split(jax.random.key(seed), 16)
    own_keys = jax.random.split(jax.random.fold_in(keys[15], part), 16)
    residual_in = gaussian(own_keys[0], (TOKENS, D), 1.0, 6.0, ((0, 8),))
    queries = draw_queries(jax.random.fold_in(jax.random.fold_in(keys[15], part), 71), part)
    key_cache = draw_key_cache(jax.random.fold_in(jax.random.fold_in(keys[15], part), 71), part)
    value_cache = gaussian(own_keys[3], (SEQS, PREFIX, KVH, HD), 1.0, 6.0, ((0, 8), (2, 2)))
    new_keys = gaussian(own_keys[4], (TOKENS, KVH, HD), 1.0, 6.0, ((0, 8), (1, 2)))
    new_values = gaussian(own_keys[5], (TOKENS, KVH, HD), 1.0, 6.0, ((0, 8), (1, 2)))
    prefix_len = draw_prefix_len(jax.random.fold_in(jax.random.fold_in(keys[15], part), 71), part)
    o_weight = gaussian(keys[7], (QH * HD, D), (QH * HD) ** -0.5, 0.078125, ((0, 2), (1, 8)))
    norm_gain = jnp.clip(1.0 + 0.1 * jax.random.normal(keys[8], (D,), jnp.float32), 0.5, 1.5)
    expert_ids_keys = jax.random.split(jax.random.fold_in(own_keys[9], 1), TOKENS // TOK_DEV)
    expert_ids_turns = jax.random.permutation(jax.random.fold_in(own_keys[9], 3), TOKENS // TOK_DEV)
    expert_ids = jax.vmap(lambda own, number: routed_block(jax.random.fold_in(own_keys[9], 2), own, number, TOK_DEV, EXPERTS, TOP, CAP, 1))(expert_ids_keys, expert_ids_turns).reshape((TOKENS, TOP))
    route_weights = jnp.clip(0.1 + 0.3 * jax.random.uniform(own_keys[10], (TOKENS, TOP), jnp.float32) ** block_scale(own_keys[10], (TOKENS, TOP), ((0, 8),), -0.2, 0.2), 0.1, 0.4)
    capacity = draw_capacity(jax.random.fold_in(jax.random.fold_in(keys[15], part), 71), part)
    gate_w = gaussian(keys[12], (EXPERTS, D, FF), D ** -0.5, 0.09375, ((0, 8), (2, 2)))
    up_w = gaussian(keys[13], (EXPERTS, D, FF), D ** -0.5, 0.09375, ((0, 8), (2, 2)))
    down_w = gaussian(keys[14], (EXPERTS, FF, D), FF ** -0.5, 0.15625, ((0, 8), (1, 2)))
    return {"residual_in": residual_in, "queries": queries, "key_cache": key_cache, "value_cache": value_cache, "new_keys": new_keys, "new_values": new_values, "prefix_len": prefix_len, "o_weight": o_weight, "norm_gain": norm_gain, "expert_ids": expert_ids, "route_weights": route_weights, "capacity": capacity, "gate_w": gate_w, "up_w": up_w, "down_w": down_w}


def attend(rows_q, prefix_keys, prefix_values, fresh_keys, fresh_values, length, group_size):
    row_count = rows_q.shape[0]
    score_scale = rows_q.shape[1] ** (-0.5)
    prefix_scores = jnp.dot(rows_q, prefix_keys.T, preferred_element_type=jnp.float32) * score_scale
    fresh_scores = jnp.dot(rows_q, fresh_keys.T, preferred_element_type=jnp.float32) * score_scale
    prefix_valid = jnp.arange(prefix_keys.shape[0])[None, :] < length
    query_pos = jnp.arange(row_count) // group_size
    fresh_valid = jnp.arange(fresh_keys.shape[0])[None, :] <= query_pos[:, None]
    prefix_scores = jnp.where(prefix_valid, prefix_scores, -1e+30)
    fresh_scores = jnp.where(fresh_valid, fresh_scores, -1e+30)
    highest = jnp.maximum(lax.optimization_barrier(jnp.max(prefix_scores, 1)), lax.optimization_barrier(jnp.max(fresh_scores, 1)))[:, None]
    prefix_prob = jnp.exp(prefix_scores - highest)
    fresh_prob = jnp.exp(fresh_scores - highest)
    running = lax.optimization_barrier(jnp.sum(prefix_prob, 1)) + lax.optimization_barrier(jnp.sum(fresh_prob, 1))
    summed = jnp.dot(prefix_prob.astype(jnp.bfloat16), prefix_values, preferred_element_type=jnp.float32)
    summed = summed + jnp.dot(fresh_prob.astype(jnp.bfloat16), fresh_values, preferred_element_type=jnp.float32)
    return (summed / running[:, None]).astype(jnp.bfloat16)

def reference(residual_in, queries, key_cache, value_cache, new_keys, new_values, prefix_len, o_weight, norm_gain, expert_ids, route_weights, capacity, gate_w, up_w, down_w):
    group_size = QH // KVH

    def per_sequence(operands):
        seq_queries, seq_keys, seq_values, seq_new_keys, seq_new_values, length = operands
        pieces = []
        for kv_head in range(KVH):
            block_q = seq_queries[:, kv_head * group_size:(kv_head + 1) * group_size].reshape(RESP * group_size, HD)
            attended = attend(block_q, seq_keys[:, kv_head], seq_values[:, kv_head], seq_new_keys[:, kv_head], seq_new_values[:, kv_head], length, group_size)
            pieces.append(attended.reshape(RESP, group_size, HD))
        return jnp.concatenate(pieces, 1)
    attended_all = lax.map(per_sequence, (queries.reshape(SEQS, RESP, QH, HD), key_cache, value_cache, new_keys.reshape(SEQS, RESP, KVH, HD), new_values.reshape(SEQS, RESP, KVH, HD), prefix_len))
    attended_flat = attended_all.reshape(TOKENS, QH * HD)
    projected = jnp.dot(attended_flat, o_weight, preferred_element_type=jnp.float32).astype(jnp.bfloat16)
    hidden = (residual_in.astype(jnp.float32) + projected.astype(jnp.float32)).astype(jnp.bfloat16)
    hidden_wide = hidden.astype(jnp.float32)
    normed = (hidden_wide * lax.rsqrt(lax.optimization_barrier(jnp.mean(hidden_wide * hidden_wide, 1, keepdims=True)) + 1e-05) * norm_gain[None, :]).astype(jnp.bfloat16)
    route_expert = expert_ids.reshape(-1)
    onehot = (route_expert[:, None] == jnp.arange(EXPERTS)[None, :]).astype(jnp.int32)
    global_rank = lax.optimization_barrier(jnp.sum((jnp.cumsum(onehot, 0) - onehot) * onehot, 1))
    blocked = onehot.reshape(N_DEV, TOK_DEV * TOP, EXPERTS)
    local_rank = lax.optimization_barrier(jnp.sum((jnp.cumsum(blocked, 1) - blocked) * blocked, 2)).reshape(-1)
    route_limit = lax.optimization_barrier(jnp.sum(onehot * capacity[None, :], 1))
    retained = global_rank < route_limit
    source_dev = jnp.arange(TOKENS * TOP) // (TOK_DEV * TOP)
    slot_index = (route_expert * (N_DEV * CAP) + source_dev * CAP + local_rank).astype(jnp.int32)
    target_slot = jnp.where(retained, slot_index, EXPERTS * N_DEV * CAP).astype(jnp.int32)
    token_index = (jnp.arange(TOKENS * TOP) // TOP).astype(jnp.int32)
    slot_token = jnp.full((EXPERTS * N_DEV * CAP + 1,), TOKENS, jnp.int32).at[target_slot].set(token_index)[:EXPERTS * N_DEV * CAP]
    padded = jnp.concatenate([normed, jnp.zeros((1, D), jnp.bfloat16)], 0)
    expert_rows = padded[slot_token].reshape(EXPERTS, N_DEV * CAP, D)
    half_units = FF // N_HEAD

    def run_expert(operands):
        rows_in, gate_weight, up_weight, down_weight = operands
        gate_act = jnp.dot(rows_in, gate_weight, preferred_element_type=jnp.float32)
        up_act = jnp.dot(rows_in, up_weight, preferred_element_type=jnp.float32)
        activated = (jax.nn.silu(gate_act) * up_act).astype(jnp.bfloat16)
        running = jnp.zeros((rows_in.shape[0], D), jnp.float32)
        for half_block in range(N_HEAD):
            partial_value = jnp.dot(activated[:, half_block * half_units:(half_block + 1) * half_units], down_weight[half_block * half_units:(half_block + 1) * half_units], preferred_element_type=jnp.float32)
            running = running + partial_value.astype(jnp.bfloat16).astype(jnp.float32)
        return running.astype(jnp.bfloat16)
    expert_out = lax.map(run_expert, (expert_rows, gate_w, up_w, down_w))
    route_rows = expert_out.reshape(-1, D)[slot_index]
    route_scale = jnp.where(retained, route_weights.reshape(-1), 0.0)
    moe_out = lax.optimization_barrier(jnp.sum((route_rows.astype(jnp.float32) * route_scale[:, None]).reshape(TOKENS, TOP, D), 1)).astype(jnp.bfloat16)
    return (hidden, moe_out)
```

```python
import functools

import jax
import jax.numpy as jnp
from jax import lax
from jax.experimental import pallas as pl
from jax.experimental.pallas import tpu as pltpu
from jax.sharding import PartitionSpec as P

VMEM = 56 << 20


def cost(flops, moved, trans=0):
    return pl.CostEstimate(flops=int(flops), bytes_accessed=int(moved), transcendentals=int(trans))


def attend_body(len_ref, q_ref, k_ref, v_ref, nk_ref, nv_ref, o_ref, *, seq, heads, step):
    tok = q_ref.shape[0]
    hd = q_ref.shape[1] // heads
    length = len_ref[seq]
    keys, values, fresh_keys, fresh_values = k_ref[...], v_ref[...], nk_ref[...], nv_ref[...]
    scale = hd ** (-0.5)
    count = keys.shape[0]
    last = (((1,), (1,)), ((), ()))
    for h in range(0, heads, step):
        q = jnp.concatenate([q_ref[:, (h + i) * hd : (h + i + 1) * hd] for i in range(step)], 0)
        s = lax.dot_general(q, keys, last, preferred_element_type=jnp.float32)
        f = lax.dot_general(q, fresh_keys, last, preferred_element_type=jnp.float32)
        s = jnp.where(lax.broadcasted_iota(jnp.int32, (1, count), 1) < length, s, -1e30)
        row = lax.broadcasted_iota(jnp.int32, f.shape, 0) % tok
        f = jnp.where(lax.broadcasted_iota(jnp.int32, f.shape, 1) <= row, f, -1e30)
        m = jnp.maximum(jnp.max(s, 1, keepdims=True), jnp.max(f, 1, keepdims=True))
        p = jnp.exp((s - m) * scale)
        pf = jnp.exp((f - m) * scale)
        total = jnp.sum(p, 1, keepdims=True) + jnp.sum(pf, 1, keepdims=True)
        o = jnp.dot(p.astype(jnp.bfloat16), values, preferred_element_type=jnp.float32)
        o = o + jnp.dot(pf.astype(jnp.bfloat16), fresh_values, preferred_element_type=jnp.float32)
        o = (o / total).astype(jnp.bfloat16)
        for i in range(step):
            o_ref[:, (h + i) * hd : (h + i + 1) * hd] = o[i * tok : (i + 1) * tok]


def attend(q, keys, values, fresh_keys, fresh_values, lengths, seq, hd):
    tok, wide = q.shape
    count, kvw = keys.shape
    kv = kvw // hd
    heads = wide // hd // kv
    step = 2 if heads % 2 == 0 else 1
    return pl.pallas_call(
        functools.partial(attend_body, seq=seq, heads=heads, step=step),
        out_shape=jax.ShapeDtypeStruct((tok, wide), jnp.bfloat16),
        grid_spec=pltpu.PrefetchScalarGridSpec(
            num_scalar_prefetch=1,
            grid=(kv,),
            in_specs=[
                pl.BlockSpec((tok, heads * hd), lambda h, l: (0, h)),
                pl.BlockSpec((count, hd), lambda h, l: (0, h)),
                pl.BlockSpec((count, hd), lambda h, l: (0, h)),
                pl.BlockSpec((tok, hd), lambda h, l: (0, h)),
                pl.BlockSpec((tok, hd), lambda h, l: (0, h)),
            ],
            out_specs=pl.BlockSpec((tok, heads * hd), lambda h, l: (0, h)),
        ),
        compiler_params=pltpu.CompilerParams(vmem_limit_bytes=VMEM),
        cost_estimate=cost(4 * tok * wide * count, 2 * count * kvw * 2, tok * wide // hd * count),
        name="attend",
    )(lengths, q, keys, values, fresh_keys, fresh_values)


def project_body(order_ref, w_ref, *refs):
    slots, (keep_ref, send_ref) = refs[:-2], refs[-2:]
    head = order_ref[len(slots)]
    rows = slots[0].shape[0]
    half = rows // 2
    x = jnp.concatenate([s[...] for s in slots], 0)
    out = jnp.dot(x, w_ref[...], preferred_element_type=jnp.float32)
    for j in range(len(slots)):
        first = out[j * rows : j * rows + half]
        second = out[j * rows + half : (j + 1) * rows]
        keep_ref[order_ref[j]] = jnp.where(head == 0, first, second)
        send_ref[order_ref[j]] = jnp.where(head == 0, second, first).astype(jnp.bfloat16)


def project(slots, w, order):
    n = len(slots)
    rows, depth = slots[0].shape
    cols = w.shape[1]
    whole = lambda a: pl.BlockSpec(a.shape, lambda i, o: (0,) * a.ndim)
    shape = (n, rows // 2, cols)
    return pl.pallas_call(
        project_body,
        out_shape=(jax.ShapeDtypeStruct(shape, jnp.float32), jax.ShapeDtypeStruct(shape, jnp.bfloat16)),
        grid_spec=pltpu.PrefetchScalarGridSpec(
            num_scalar_prefetch=1,
            grid=(1,),
            in_specs=[whole(w)] + [whole(s) for s in slots],
            out_specs=[pl.BlockSpec(shape, lambda i, o: (0, 0, 0))] * 2,
        ),
        compiler_params=pltpu.CompilerParams(vmem_limit_bytes=VMEM),
        cost_estimate=cost(2 * n * rows * depth * cols, 2 * (n * rows * depth + depth * cols)),
        name="project",
    )(order, w, *slots)


def gate_up_body(order_ref, wt_ref, gain_a, gain_b, ga_ref, gb_ref, ua_ref, ub_ref, *refs, n, eps):
    own, other = refs[:n], refs[n : 2 * n]
    act_ref, hid_ref, xs, gacc, uacc, ss = refs[2 * n :]
    e, k = pl.program_id(0), pl.program_id(1)
    ksteps = pl.num_programs(1)
    me, head = order_ref[n], order_ref[n + 1]
    _, part, cw = own[0].shape
    rows = 2 * n * part
    half = n // 2

    @pl.when(e == 0)
    def _():
        for step in range(n // 2):

            @pl.when(k == step)
            def _(step=step):
                total = jnp.zeros((rows, 1), jnp.float32)
                for i, gain in ((0, gain_a), (1, gain_b)):
                    j = 2 * step + i
                    v = jnp.concatenate([own[j][...], other[j][...]], 0).reshape(rows, cw)
                    v = v.astype(jnp.float32)
                    total = total + jnp.sum(v * v, axis=1, keepdims=True)
                    xs[j] = (v * gain[...]).astype(jnp.bfloat16)
                    c = order_ref[j]

                    @pl.when(c // half == head)
                    def _(c=c, j=j):
                        at = pl.ds(pl.multiple_of((c % half) * cw, cw), cw)
                        hid_ref[0, :, at] = own[j][me]
                        hid_ref[1, :, at] = other[j][me]

                if step == 0:
                    ss[...] = total
                else:
                    ss[...] += total

    last = (((1,), (1,)), ((), ()))
    xa, xb = xs[2 * k], xs[2 * k + 1]
    mm = lambda a, b: lax.dot_general(a, b, last, preferred_element_type=jnp.float32)
    g = mm(xa, ga_ref[...]) + mm(xb, gb_ref[...])
    u = mm(xa, ua_ref[...]) + mm(xb, ub_ref[...])

    @pl.when(k == 0)
    def _():
        gacc[...] = g
        uacc[...] = u

    @pl.when((k > 0) & (k < ksteps - 1))
    def _():
        gacc[...] += g
        uacc[...] += u

    @pl.when(k == ksteps - 1)
    def _():
        r = lax.rsqrt(ss[...] / (n * cw) + eps)
        gg = (gacc[...] + g) * r
        uu = (uacc[...] + u) * r
        wt = wt_ref[...]
        lane = lax.broadcasted_iota(jnp.int32, wt.shape, 1)
        w = jnp.sum(jnp.where(lane == e, wt, 0.0), axis=1, keepdims=True)
        act_ref[...] = (gg / (1 + jnp.exp(-gg)) * (uu * w)).astype(jnp.bfloat16)


def gate_up(own, other, wt, gain, gate_t, up_t, order):
    n = len(own)
    _, part, cw = own[0].shape
    experts, ff, depth = gate_t.shape
    rows = 2 * n * part
    whole = lambda a: pl.BlockSpec(a.shape, lambda e, k, o: (0,) * a.ndim, pipeline_mode=pl.Buffered(1))
    weight = lambda i: pl.BlockSpec((None, ff, cw), lambda e, k, o: (e, 0, o[2 * k + i]))
    gains = lambda i: pl.BlockSpec((1, cw), lambda e, k, o: (0, o[2 * k + i]))
    return pl.pallas_call(
        functools.partial(gate_up_body, n=n, eps=1e-5),
        out_shape=(
            jax.ShapeDtypeStruct((experts, rows, ff), jnp.bfloat16),
            jax.ShapeDtypeStruct((2, part, n // 2 * cw), jnp.bfloat16),
        ),
        grid_spec=pltpu.PrefetchScalarGridSpec(
            num_scalar_prefetch=1,
            grid=(experts, n // 2),
            in_specs=[whole(wt), gains(0), gains(1), weight(0), weight(1), weight(0), weight(1)]
            + [whole(a) for a in own]
            + [whole(a) for a in other],
            out_specs=[
                pl.BlockSpec((None, rows, ff), lambda e, k, o: (e, 0, 0)),
                pl.BlockSpec((2, part, n // 2 * cw), lambda e, k, o: (0, 0, 0)),
            ],
            scratch_shapes=[
                pltpu.VMEM((n, rows, cw), jnp.bfloat16),
                pltpu.VMEM((rows, ff), jnp.float32),
                pltpu.VMEM((rows, ff), jnp.float32),
                pltpu.VMEM((rows, 1), jnp.float32),
            ],
        ),
        compiler_params=pltpu.CompilerParams(vmem_limit_bytes=VMEM),
        cost_estimate=cost(4 * rows * depth * ff * experts, 4 * depth * ff * experts),
        name="gate_up",
    )(order, wt, gain, gain, gate_t, gate_t, up_t, up_t, *own, *other)


def down_body(at_ref, act_ref, w_ref, o_ref):
    acc = jnp.dot(act_ref[0], w_ref[0], preferred_element_type=jnp.float32)
    for e in range(1, act_ref.shape[0]):
        acc = acc + jnp.dot(act_ref[e], w_ref[e], preferred_element_type=jnp.float32)
    o_ref[...] = acc.reshape(o_ref.shape).astype(o_ref.dtype)


def down(act, w, half, n):
    experts, rows, ff = act.shape
    cols = w.shape[2] // 2
    nb = min(1024, cols)
    steps = cols // nb
    part = rows // (2 * n)
    return pl.pallas_call(
        down_body,
        out_shape=jax.ShapeDtypeStruct((2, n, part, cols), jnp.bfloat16),
        grid_spec=pltpu.PrefetchScalarGridSpec(
            num_scalar_prefetch=1,
            grid=(steps,),
            in_specs=[
                pl.BlockSpec(act.shape, lambda i, h: (0, 0, 0)),
                pl.BlockSpec((experts, ff, nb), lambda i, h: (0, 0, h[0] * steps + i)),
            ],
            out_specs=pl.BlockSpec((2, n, part, nb), lambda i, h: (0, 0, 0, i)),
        ),
        compiler_params=pltpu.CompilerParams(vmem_limit_bytes=VMEM),
        cost_estimate=cost(2 * rows * ff * experts * cols, 2 * (ff * experts * cols + rows * cols)),
        name="down",
    )(half, act, w)


def on_device(
    residual_in, queries, key_cache, value_cache, new_keys, new_values, prefix_len, o_weight,
    norm_gain, expert_ids, route_weights, capacity, gate_w, up_w, down_w, *, nz, ny,
):
    n = nz * ny
    d, head = lax.axis_index("dev"), lax.axis_index("head")
    z, y = d // ny, d % ny
    tok, q_heads, hd = queries.shape
    seqs = key_cache.shape[0]
    resp = tok // seqs
    part = resp // 2
    f32, bf16 = jnp.float32, jnp.bfloat16
    ring = [(a * ny + b, (a + 1) % nz * ny + b) for a in range(nz) for b in range(ny)]
    swap = [(a * ny + b, a * ny + (b + 1) % ny) for a in range(nz) for b in range(ny)]
    pass_on = lambda x: lax.ppermute(x, "dev", ring)
    across = lambda x: lax.ppermute(x, "dev", swap)
    partner = lambda x: lax.ppermute(x, "head", [(0, 1), (1, 0)])

    def gather(x):
        line = [x]
        for _ in range(nz - 1):
            line.append(pass_on(line[-1]))
        if ny == 1:
            return line
        return [v for x in line for v in (x, across(x))]

    slot_dev = jnp.stack([(z - j) % nz * ny + (y + i) % ny for j in range(nz) for i in range(ny)])
    order = jnp.concatenate([slot_dev, jnp.stack([d, head])]).astype(jnp.int32)
    order_p = jnp.concatenate([slot_dev, head[None]]).astype(jnp.int32)

    packed = jnp.concatenate([expert_ids.astype(f32), route_weights], 1)
    pair = packed[None] if ny == 1 else jnp.stack([packed, across(packed)])
    line = [pair]
    for _ in range(nz - 1):
        line.append(pass_on(line[-1]))
    got = jnp.concatenate(line, 0)
    table = jnp.zeros((n, tok, packed.shape[1]), f32).at[slot_dev].set(got).reshape(n * tok, -1)
    top = expert_ids.shape[1]
    ids, weights = table[:, :top].astype(jnp.int32), table[:, top:]
    local = gate_w.shape[0]
    mine = d * local + jnp.arange(local)
    hits = ids[:, :, None] == mine[None, None, :]
    named = jnp.any(hits, 1)
    earlier = jnp.cumsum(named.astype(jnp.int32), 0) - named
    limit = lax.dynamic_slice_in_dim(capacity, d * local, local)
    wt = jnp.where(earlier < limit[None], jnp.sum(jnp.where(hits, weights[:, :, None], 0.0), 1), 0.0)
    wt = wt.reshape(n, seqs, 2, part, local).transpose(1, 2, 0, 3, 4)
    wt = jnp.where(head == 0, wt, wt[:, ::-1]).reshape(seqs, 2 * n * part, local)

    width = residual_in.shape[1]
    cw = width // n
    res = residual_in.reshape(seqs, 2, part, width)
    res = lax.dynamic_index_in_dim(res, head, 1, False).reshape(seqs, part, n, cw)
    res = lax.all_to_all(res.transpose(2, 0, 1, 3), "dev", split_axis=0, concat_axis=0, tiled=True)

    gain = norm_gain[None]
    gate_t, up_t = gate_w.swapaxes(1, 2), up_w.swapaxes(1, 2)
    q_flat = queries.reshape(seqs, resp, q_heads * hd)
    head1 = head.astype(jnp.int32)[None]
    hidden_parts, moe_parts = [], []
    for s in range(seqs):
        flat = lambda x: x.reshape(x.shape[0], -1)
        rows = slice(s * resp, (s + 1) * resp)
        att = attend(
            q_flat[s], flat(key_cache[s]), flat(value_cache[s]), flat(new_keys[rows]),
            flat(new_values[rows]), prefix_len, s, hd,
        )
        keep, send = project(gather(att), o_weight, order_p)
        projected = (keep + partner(send).astype(f32)).astype(bf16)
        hidden = (res[:, s].astype(f32) + projected.astype(f32)).astype(bf16)
        own = gather(hidden)
        other = [partner(v) for v in own]
        act, hid = gate_up(own, other, wt[s], gain, gate_t, up_t, order)
        hidden_parts.append(hid)
        theirs = partner(down(act, down_w, 1 - head1, n))
        ours = down(act, down_w, head1, n)

        def block(zz, yy):
            at = zz % nz * ny + yy % ny
            take = lambda a: lax.dynamic_index_in_dim(a, at, 1, False)
            return take(ours).astype(f32) + take(theirs)[::-1].astype(f32)

        running = None
        for j in range(1, nz + 1):
            term = block(z - j, y)
            if ny > 1:
                term = term + across(block(z - j, y + 1).astype(bf16)).astype(f32)
            if running is not None:
                term = term + running.astype(f32)
            running = term.astype(bf16)
            if j < nz:
                running = pass_on(running)
        moe_parts.append(running)
    place = lambda parts: jnp.stack([jnp.where(head == 0, p, p[::-1]) for p in parts]).reshape(tok, -1)
    return place(hidden_parts), place(moe_parts)


def solution(mesh):
    in_specs = (
        P(("group", "dev"), None),
        P(("group", "dev"), "head", None),
        P(("group", "dev"), None, "head", None),
        P(("group", "dev"), None, "head", None),
        P(("group", "dev"), "head", None),
        P(("group", "dev"), "head", None),
        P(("group", "dev")),
        P("head", "dev"),
        P(),
        P(("group", "dev"), None),
        P(("group", "dev"), None),
        P("group"),
        P("dev", None, "head"),
        P("dev", None, "head"),
        P("dev", "head", None),
    )
    out_specs = (P(("group", "dev"), "head"), P(("group", "dev"), "head"))
    n = mesh.shape["dev"]
    spots = [getattr(c, "coords", (0, 0, i)) for i, c in enumerate(mesh.devices[0, :, 0])]
    ny = n // len({p[2] for p in spots})
    return jax.shard_map(
        functools.partial(on_device, nz=n // ny, ny=ny),
        mesh=mesh, in_specs=in_specs, out_specs=out_specs, check_vma=False,
    )
```

```python
import functools

import jax
import jax.numpy as jnp
from jax import lax
from jax.experimental import pallas as pl
from jax.experimental.pallas import tpu as pltpu
from jax.sharding import PartitionSpec as P


VMEM = 58 << 20
LAST = (((1,), (1,)), ((), ()))


def cost(flops, moved, trans=0):
    return pl.CostEstimate(flops=int(flops), bytes_accessed=int(moved), transcendentals=int(trans))


def attend_body(len_ref, q_ref, k_ref, v_ref, nk_ref, nv_ref, o_ref, ks, vs, *, seq, kv, heads, hd, step, kb):
    tok = q_ref.shape[0]
    count = k_ref.shape[0] // kv
    length = len_ref[seq]
    c = hd ** (-0.5) * 1.4426950408889634
    n = kb * kv
    r = lax.broadcasted_iota(jnp.int32, (n, n), 0); cc = lax.broadcasted_iota(jnp.int32, (n, n), 1)
    perm = (cc == (r % kb) * kv + r // kb).astype(jnp.bfloat16)
    for b in range(count // kb):
        for src, dst in ((k_ref, ks), (v_ref, vs)):
            t = jnp.dot(perm, src[b * n:(b + 1) * n], preferred_element_type=jnp.float32).astype(jnp.bfloat16)
            for h in range(kv):
                dst[h, b * kb:(b + 1) * kb] = t[h * kb:(h + 1) * kb]
    valid = lax.broadcasted_iota(jnp.int32, (1, count), 1) < length
    for h in range(kv):
        keys, values = ks[h], vs[h]
        fk, fv = nk_ref[:, h * hd:(h + 1) * hd], nv_ref[:, h * hd:(h + 1) * hd]
        for i in range(0, heads, step):
            base = h * heads + i
            q = jnp.concatenate([q_ref[:, (base + j) * hd:(base + j + 1) * hd] for j in range(step)], 0)
            s = lax.dot_general(q, keys, LAST, preferred_element_type=jnp.float32)
            f = lax.dot_general(q, fk, LAST, preferred_element_type=jnp.float32)
            s = jnp.where(valid, s, -1e30)
            row = lax.broadcasted_iota(jnp.int32, f.shape, 0) % tok
            f = jnp.where(lax.broadcasted_iota(jnp.int32, f.shape, 1) <= row, f, -1e30)
            m = jnp.maximum(jnp.max(s, 1, keepdims=True), jnp.max(f, 1, keepdims=True))
            p = jnp.exp2((s - m) * c)
            pf = jnp.exp2((f - m) * c)
            total = jnp.sum(p, 1, keepdims=True) + jnp.sum(pf, 1, keepdims=True)
            o = jnp.dot(p.astype(jnp.bfloat16), values, preferred_element_type=jnp.float32)
            o = o + jnp.dot(pf.astype(jnp.bfloat16), fv, preferred_element_type=jnp.float32)
            o = (o / total).astype(jnp.bfloat16)
            for j in range(step):
                o_ref[:, (base + j) * hd:(base + j + 1) * hd] = o[j * tok:(j + 1) * tok]


def attend(q, keys, values, fk, fv, lengths, seq, kv, hd, step=2):
    tok, wide = q.shape
    rows = keys.shape[1]
    heads = wide // hd // kv
    whole = lambda a: pl.BlockSpec(a.shape, lambda i, l: (0,) * a.ndim)
    kspec = pl.BlockSpec((None, rows, hd), lambda i, l: (seq, 0, 0))
    return pl.pallas_call(
        functools.partial(attend_body, seq=seq, kv=kv, heads=heads, hd=hd, step=step, kb=128),
        out_shape=jax.ShapeDtypeStruct((tok, wide), jnp.bfloat16),
        grid_spec=pltpu.PrefetchScalarGridSpec(num_scalar_prefetch=1, grid=(1,),
            in_specs=[whole(q), kspec, kspec, whole(fk), whole(fv)], out_specs=whole(q),
            scratch_shapes=[pltpu.VMEM((kv, rows // kv, hd), jnp.bfloat16)] * 2),
        compiler_params=pltpu.CompilerParams(vmem_limit_bytes=VMEM),
        cost_estimate=cost(4 * tok * wide * (rows // kv), 4 * rows * hd, tok * wide // hd * (rows // kv)), name="attend")(lengths, q, keys, values, fk, fv)


def project_body(order_ref, w_ref, *refs, nz, pieces):
    slots, refs = refs[:nz], refs[nz:]
    first, second = refs[:pieces], refs[pieces : 2 * pieces]
    keep_ref, send_ref, x = refs[2 * pieces :]
    head, y, g = order_ref[nz], order_ref[nz + 1], order_ref[nz + 2]
    rows = slots[0].shape[0]
    half = rows // 2
    cw = w_ref.shape[1]
    for j in range(nz):
        x[j * rows : (j + 1) * rows] = slots[j][...]

    def put(out, at):
        for j in range(nz):
            low = out[j * rows : j * rows + half]
            high = out[j * rows + half : (j + 1) * rows]
            keep_ref[order_ref[j], :, at] = jnp.where(head == 0, low, high)
            send_ref[order_ref[j], :, at] = jnp.where(head == 0, high, low).astype(jnp.bfloat16)

    span = lambda i, size: pl.ds(pl.multiple_of(i * size, size), size)
    put(jnp.dot(x[...], w_ref[...], preferred_element_type=jnp.float32), span(y, cw))
    if pieces:
        depth = first[0].shape[0]
        out = 0.0
        for k in range(pieces):
            for w, i in ((first[k], 2 * k + g), (second[k], 2 * k + 1 - g)):
                out = out + jnp.dot(x[:, span(i, depth)], w[...], preferred_element_type=jnp.float32)
        put(out, span(1 - y, cw))


def project(slots, w, first, second, order):
    nz = len(slots)
    rows, depth = slots[0].shape
    cols = w.shape[1] * (2 if first else 1)
    whole = lambda a: pl.BlockSpec(a.shape, lambda i, o: (0,) * a.ndim)
    shape = (nz, rows // 2, cols)
    return pl.pallas_call(
        functools.partial(project_body, nz=nz, pieces=len(first)),
        out_shape=(jax.ShapeDtypeStruct(shape, jnp.float32), jax.ShapeDtypeStruct(shape, jnp.bfloat16)),
        grid_spec=pltpu.PrefetchScalarGridSpec(
            num_scalar_prefetch=1,
            grid=(1,),
            in_specs=[whole(a) for a in (w, *slots, *first, *second)],
            out_specs=[pl.BlockSpec(shape, lambda i, o: (0, 0, 0))] * 2,
            scratch_shapes=[pltpu.VMEM((nz * rows, depth), jnp.bfloat16)],
        ),
        compiler_params=pltpu.CompilerParams(vmem_limit_bytes=VMEM),
        cost_estimate=cost(2 * nz * rows * depth * cols, 2 * (nz * rows * depth + depth * cols)),
        name="project",
    )(order, w, *slots, *first, *second)


def put_rows(o_ref, acc):
    nz, _, part, nb = o_ref.shape
    for i in range(2):
        o_ref[:, i] = acc[i * nz * part:(i + 1) * nz * part].reshape(nz, part, nb).astype(o_ref.dtype)


def expert_body(order_ref, wt_ref, gain_ref, gate_ref, up_ref, down_ref, *refs, nz, nf, eps, show):
    p, refs = refs[:4], refs[4:]
    theirs_ref, acts_ref, refs = refs[0], refs[1], refs[2:]
    if show: hid_ref, refs = refs[0], refs[1:]
    xs, act_t = refs
    s = pl.program_id(0)
    head, me = order_ref[nz], order_ref[nz + 3]
    _, part, cw = p[0].shape
    rows = 2 * nz * part
    half = nz // 2
    fb = gate_ref.shape[0]
    gs = act_t.shape[0] // fb

    @pl.when(s == 0)
    def _():
        total = jnp.zeros((rows, 1), jnp.float32)
        pairs = [(p[0], p[2])] + [(p[1].at[j], p[3].at[j]) for j in range(nz - 1)]
        for j, (own, other) in enumerate(pairs):
            v = jnp.concatenate([own[...], other[...]], 0).reshape(rows, cw).astype(jnp.float32)
            total = total + jnp.sum(v * v, axis=1, keepdims=True)
            if show:
                c = order_ref[j]

                @pl.when(c // half == head)
                def _(c=c, own=own, other=other):
                    at = pl.ds(pl.multiple_of((c % half) * cw, cw), cw)
                    hid_ref[0, :, at] = own[me]
                    hid_ref[1, :, at] = other[me]
        r = lax.rsqrt(total / (nz * cw) + eps)
        for j, (own, other) in enumerate(pairs):
            at = pl.ds(pl.multiple_of(order_ref[j] * cw, cw), cw)
            v = jnp.concatenate([own[...], other[...]], 0).reshape(rows, cw).astype(jnp.float32)
            xs[:, at] = (v * r * gain_ref[:, at]).astype(jnp.bfloat16)

    @pl.when(s < gs)
    def _():
        g = lax.dot_general(gate_ref[...], xs[...], LAST, preferred_element_type=jnp.float32)
        u = lax.dot_general(up_ref[...], xs[...], LAST, preferred_element_type=jnp.float32)
        w = wt_ref[pl.ds(s // nf, 1), :]
        act_t[pl.ds(pl.multiple_of(s * fb, 16), fb), :] = (g / (1 + jnp.exp(-g)) * (u * w)).astype(jnp.bfloat16)

    @pl.when(s == gs)
    def _():
        acts_ref[...] = act_t[...].T

    @pl.when(s >= gs)
    def _():
        w = down_ref[...]
        put_rows(theirs_ref, jnp.dot(acts_ref[...], w.reshape(-1, w.shape[2]), preferred_element_type=jnp.float32))


def expert(p, wt, gain, gate_t, up_t, down_w, order, nf=2, split=2, show=True):
    nz, part, cw = p[0].shape
    experts, ff, depth = gate_t.shape
    rows = 2 * nz * part
    cols = down_w.shape[2] // 2
    nb = cols // split
    fb = ff // nf
    gs = experts * nf
    whole = lambda a: pl.BlockSpec(a.shape, lambda s, o: (0,) * a.ndim, pipeline_mode=pl.Buffered(1))

    def fi(s, o):
        t = jnp.minimum(s, gs - 1)
        return (lax.div(t, nf), lax.rem(t, nf), 0)

    weight = pl.BlockSpec((None, fb, depth), fi)

    def dcol(s, o): return (0, 0, (1 - o[nz]) * split + jnp.maximum(s - gs, 0))

    out = (nz, 2, part, cols)
    hid = (2, part, nz // 2 * cw)
    shapes = [jax.ShapeDtypeStruct(out, jnp.bfloat16), jax.ShapeDtypeStruct((rows, experts * ff), jnp.bfloat16)]
    specs = [pl.BlockSpec(out[:-1] + (nb,), lambda s, o: (0, 0, 0, jnp.maximum(s - gs, 0))),
             pl.BlockSpec((rows, experts * ff), lambda s, o: (0, 0))]
    if show:
        shapes.append(jax.ShapeDtypeStruct(hid, jnp.bfloat16)); specs.append(pl.BlockSpec(hid, lambda s, o: (0, 0, 0)))
    return pl.pallas_call(
        functools.partial(expert_body, nz=nz, nf=nf, eps=1e-5, show=show),
        out_shape=shapes,
        grid_spec=pltpu.PrefetchScalarGridSpec(num_scalar_prefetch=1, grid=(gs + split,),
            in_specs=[whole(wt), whole(gain), weight, weight, pl.BlockSpec((experts, ff, nb), dcol)] + [whole(a) for a in p],
            out_specs=specs,
            scratch_shapes=[pltpu.VMEM((rows, depth), jnp.bfloat16), pltpu.VMEM((experts * ff, rows), jnp.bfloat16)]),
        compiler_params=pltpu.CompilerParams(vmem_limit_bytes=VMEM),
        cost_estimate=cost(2 * rows * depth * ff * experts * 2.5, 5 * depth * ff * experts), name="expert")(order, wt, gain, gate_t, up_t, down_w, *p)


def down_body(order_ref, act_ref, w_ref, *refs, nz, adds, spread):
    extra, outs = refs[:adds], refs[adds:]
    w = w_ref[...]
    acc = jnp.dot(act_ref[...], w.reshape(-1, w.shape[2]), preferred_element_type=jnp.float32)
    part = act_ref.shape[0] // (2 * nz)

    def total(i):
        out = acc[i * nz * part : (i + 1) * nz * part].reshape(nz, part, acc.shape[1])
        for j, ref in enumerate(extra):
            out = out + ref[:, 1 - i if j == 0 else i].astype(jnp.float32)
        return out

    if not spread:
        for i in range(2):
            outs[0][:, i] = total(i).astype(outs[0].dtype)
        return
    outs, scratch = outs[:-1], outs[-1]
    for i in range(2):
        scratch[:, i] = total(i)
    for j, out in enumerate(outs):
        out[...] = scratch[lax.rem(order_ref[nz + 3] + j, nz)].astype(out.dtype)


def down(acts, down_w, order, nz, extra, spread, split=2):
    experts, ff, width = down_w.shape
    rows = acts.shape[0]
    cols = width // 2
    nb = cols // split
    part = rows // (2 * nz)
    block = pl.BlockSpec((nz, 2, part, nb), lambda i, o: (0, 0, 0, i))
    if spread:
        shapes = [jax.ShapeDtypeStruct((2, part, cols), jnp.bfloat16)] * nz
        specs = [pl.BlockSpec((2, part, nb), lambda i, o: (0, 0, i))] * nz
    else:
        shapes, specs = [jax.ShapeDtypeStruct((nz, 2, part, cols), jnp.bfloat16)], [block]
    return pl.pallas_call(
        functools.partial(down_body, nz=nz, adds=len(extra), spread=spread),
        out_shape=shapes,
        grid_spec=pltpu.PrefetchScalarGridSpec(
            num_scalar_prefetch=1,
            grid=(split,),
            in_specs=[
                pl.BlockSpec(acts.shape, lambda i, o: (0, 0)),
                pl.BlockSpec((experts, ff, nb), lambda i, o: (0, 0, o[nz] * split + i)),
            ]
            + [block] * len(extra),
            out_specs=specs,
            scratch_shapes=[pltpu.VMEM((nz, 2, part, nb), jnp.float32)] if spread else [],
        ),
        compiler_params=pltpu.CompilerParams(vmem_limit_bytes=VMEM),
        cost_estimate=cost(2 * rows * ff * experts * cols, 2 * experts * ff * cols + 2 * rows * cols),
        name="down",
    )(order, acts, down_w, *extra)


def on_device(
    residual_in, queries, key_cache, value_cache, new_keys, new_values, prefix_len, o_weight,
    norm_gain, expert_ids, route_weights, capacity, gate_w, up_w, down_w, *, nz, ny,
):
    n = nz * ny
    d, head, g = lax.axis_index("dev"), lax.axis_index("head"), lax.axis_index("group")
    z, y = d // ny, d % ny
    tok, q_heads, hd = queries.shape
    seqs = key_cache.shape[0]
    resp = tok // seqs
    part = resp // 2
    f32, bf16 = jnp.float32, jnp.bfloat16

    def shift(x, k):
        pairs = [(a * ny + b, (a + k) % nz * ny + b) for a in range(nz) for b in range(ny)]
        return lax.ppermute(x, "dev", pairs)

    def across(x):
        return lax.ppermute(x, "dev", [(a * ny + b, a * ny + (b + 1) % ny) for a in range(nz) for b in range(ny)])

    partner = lambda x: lax.ppermute(x, "head", [(0, 1), (1, 0)])
    groups = lax.axis_size("group")
    twin = lambda x: lax.ppermute(x, "group", [(i, i ^ 1) for i in range(groups)])

    slot_z = jnp.stack([(z - j) % nz for j in range(nz)])
    order = jnp.concatenate([slot_z, jnp.stack([head, y, g % 2, z])]).astype(jnp.int32)

    first, second = [], []
    if ny > 1:
        depth = o_weight.shape[0] // 4
        for k in range(2):
            first.append(across(lax.dynamic_slice_in_dim(o_weight, (2 * k + g % 2) * depth, depth, 0)))
            second.append(twin(first[-1]))

    width = residual_in.shape[1]
    cw = width // nz
    res = lax.dynamic_index_in_dim(residual_in.reshape(seqs, 2, part, width), head, 1, False)
    columns = lambda zz: lax.dynamic_slice_in_dim(res, zz % nz * cw, cw, 2)

    def line(x):
        forward, back = nz // 2, nz - 1 - nz // 2
        up, down_ = [x], [x]
        for i in range(max(forward, back)):
            if i < forward:
                up.append(shift(up[-1], 1))
            if i < back:
                down_.append(shift(down_[-1], -1))
        return up + down_[:0:-1]

    res_slots = jnp.stack([columns(z)] + [shift(columns(z + k), k) for k in range(1, nz)])
    res_line = jnp.stack([lax.dynamic_index_in_dim(res_slots, (z - a) % nz, 0, False) for a in range(nz)])

    q_flat = queries.reshape(seqs, resp, q_heads * hd)
    flat = lambda x: x.reshape(x.shape[0], -1)
    kv = key_cache.shape[2]
    keys, values = (c.reshape(seqs, -1, hd) for c in (key_cache, value_cache))
    lines = []
    for s in range(seqs):
        rows = slice(s * resp, (s + 1) * resp)
        att = attend(q_flat[s], keys, values, flat(new_keys[rows]), flat(new_values[rows]), prefix_len, s, kv, hd)
        lines.append(line(att))

    packed = jnp.concatenate([expert_ids.astype(f32), route_weights], 1)
    pair = packed[None] if ny == 1 else jnp.stack([packed, across(packed)])
    got = jnp.concatenate([pair] + [shift(pair, k) for k in range(1, nz)], 0)

    slot_dev = jnp.stack([(z - j) % nz * ny + (y + i) % ny for j in range(nz) for i in range(ny)])
    table = jnp.zeros((n, tok, packed.shape[1]), f32).at[slot_dev].set(got).reshape(n * tok, -1)
    top = expert_ids.shape[1]
    ids, weights = table[:, :top].astype(jnp.int32), table[:, top:]
    local = gate_w.shape[0]
    mine = d * local + jnp.arange(local)
    hits = ids[:, :, None] == mine[None, None, :]
    named = jnp.any(hits, 1)
    earlier = jnp.cumsum(named.astype(jnp.int32), 0) - named
    limit = lax.dynamic_slice_in_dim(capacity, d * local, local)
    wt = jnp.where(earlier < limit[None], jnp.sum(jnp.where(hits, weights[:, :, None], 0.0), 1), 0.0)
    wt = wt.reshape(nz, ny, seqs, 2, part, local).transpose(1, 2, 5, 3, 0, 4)
    wt = jnp.where(head == 0, wt, wt[:, :, :, ::-1]).reshape(ny, seqs, local, 2 * nz * part)
    wt = [lax.dynamic_index_in_dim(wt, (y + i) % ny, 0, False) for i in range(ny)]

    gain = norm_gain[None]
    gate_t, up_t = gate_w.swapaxes(1, 2), up_w.swapaxes(1, 2)
    tie = lambda a, b: lax.optimization_barrier((a, b))[0]

    planes = []
    for s in range(seqs):
        keep, send = project(lines[s], o_weight, first, second, order)
        if planes:
            keep = tie(keep, planes[-1][0][0])
        projected = (keep + partner(send).astype(f32)).astype(bf16)
        hidden = (res_line[:, s].astype(f32) + projected.astype(f32)).astype(bf16)
        later = jnp.stack(line(hidden)[1:])
        rows_of = [(hidden, later)]
        if ny > 1:
            head_part = across(hidden)
            rows_of.append((head_part, across(later)))
        pieces = []
        for a, b in rows_of:
            pa = partner(a)
            pieces.append((a, b, pa, partner(b)))
        planes.append(pieces)

    hidden_parts, moe_parts = [None] * seqs, [None] * seqs
    summed = {}

    def run(s, i, after=None):
        pieces = planes[s][i]
        if after is not None:
            pieces = (tie(pieces[0], after), *pieces[1:])
        out = expert(pieces, wt[i][s], gain, gate_t, up_t, down_w, order, show=i == 0)
        if i == 0:
            hidden_parts[s] = out[2]
        summed[s, i] = (partner(out[0]), out[1])

    def other_plane(s):
        theirs, acts = summed[s, 1]
        (mine,) = down(acts, down_w, order, nz, (theirs,), False)
        summed[s, 1] = across(mine)
        return mine

    def finish(s):
        theirs, acts = summed[s, 0]
        extra = (theirs,) + ((summed[s, 1],) if ny > 1 else ())
        terms = down(acts, down_w, order, nz, extra, True)
        moved = {}
        for step, count in ((1, nz // 2), (-1, nz - 1 - nz // 2)):
            for i, k in enumerate(range(count, 0, -1)):
                term = terms[step * k]
                if i:
                    term = (term.astype(f32) + moved[step].astype(f32)).astype(bf16)
                moved[step] = shift(term, step)
        final = terms[0].astype(f32)
        for got in moved.values():
            final = final + got.astype(f32)
        moe_parts[s] = final.astype(bf16)
        return terms[0]

    if ny == 1:
        for s in range(seqs):
            run(s, 0)
            finish(s)
    else:
        for s in range(seqs):
            first_plane = 1 if s and s == seqs - 1 else 0
            run(s, first_plane)
            if first_plane:
                other_plane(s)
            run(s, 1 - first_plane)
            if not first_plane:
                other_plane(s)
            finish(s)
    place = lambda parts: jnp.stack([jnp.where(head == 0, p, p[::-1]) for p in parts]).reshape(tok, -1)
    return place(hidden_parts), place(moe_parts)


def solution(mesh):
    in_specs = (
        P(("group", "dev"), None),
        P(("group", "dev"), "head", None),
        P(("group", "dev"), None, "head", None),
        P(("group", "dev"), None, "head", None),
        P(("group", "dev"), "head", None),
        P(("group", "dev"), "head", None),
        P(("group", "dev")),
        P("head", "dev"),
        P(),
        P(("group", "dev"), None),
        P(("group", "dev"), None),
        P("group"),
        P("dev", None, "head"),
        P("dev", None, "head"),
        P("dev", "head", None),
    )
    out_specs = (P(("group", "dev"), "head"), P(("group", "dev"), "head"))
    n = mesh.shape["dev"]
    spots = [getattr(c, "coords", (0, 0, i)) for i, c in enumerate(mesh.devices[0, :, 0])]
    ny = n // len({p[2] for p in spots})

    def body(*args):
        return on_device(*args, nz=n // ny, ny=ny)

    return jax.shard_map(body, mesh=mesh, in_specs=in_specs, out_specs=out_specs, check_vma=False)
```

```python
import functools

import jax
import jax.numpy as jnp
from jax import lax
from jax.experimental import pallas as pl
from jax.experimental.pallas import tpu as pltpu
from jax.sharding import PartitionSpec as P


VMEM = 58 << 20
LAST = (((1,), (1,)), ((), ()))


def cost(flops, moved, trans=0):
    return pl.CostEstimate(flops=int(flops), bytes_accessed=int(moved), transcendentals=int(trans))


def attend_body(len_ref, q_ref, k_ref, v_ref, nk_ref, nv_ref, o_ref, ks, vs, *, seq, kv, heads, hd, step, kb):
    tok = q_ref.shape[0]
    count = k_ref.shape[0] // kv
    length = len_ref[seq]
    c = hd ** (-0.5) * 1.4426950408889634
    n = kb * kv
    r = lax.broadcasted_iota(jnp.int32, (n, n), 0); cc = lax.broadcasted_iota(jnp.int32, (n, n), 1)
    perm = (cc == (r % kb) * kv + r // kb).astype(jnp.bfloat16)
    for b in range(count // kb):
        for src, dst in ((k_ref, ks), (v_ref, vs)):
            t = jnp.dot(perm, src[b * n:(b + 1) * n], preferred_element_type=jnp.float32).astype(jnp.bfloat16)
            for h in range(kv):
                dst[h, b * kb:(b + 1) * kb] = t[h * kb:(h + 1) * kb]
    valid = lax.broadcasted_iota(jnp.int32, (1, count), 1) < length
    wide = step * hd
    row = lax.broadcasted_iota(jnp.int32, (step * tok, tok), 0) % tok
    seen = lax.broadcasted_iota(jnp.int32, (step * tok, tok), 1) <= row

    def one(i, _):
        h = i * step // heads
        at = pl.ds(pl.multiple_of(i * wide, wide), wide)
        mine = pl.ds(pl.multiple_of(h * hd, hd), hd)
        q = q_ref[:, at]
        q = jnp.concatenate([q[:, j * hd : (j + 1) * hd] for j in range(step)], 0)
        s = lax.dot_general(q, ks[h], LAST, preferred_element_type=jnp.float32)
        f = lax.dot_general(q, nk_ref[:, mine], LAST, preferred_element_type=jnp.float32)
        s = jnp.where(valid, s, -1e30)
        f = jnp.where(seen, f, -1e30)
        m = jnp.maximum(jnp.max(s, 1, keepdims=True), jnp.max(f, 1, keepdims=True))
        p = jnp.exp2((s - m) * c)
        pf = jnp.exp2((f - m) * c)
        total = jnp.sum(p, 1, keepdims=True) + jnp.sum(pf, 1, keepdims=True)
        o = jnp.dot(p.astype(jnp.bfloat16), vs[h], preferred_element_type=jnp.float32)
        o = o + jnp.dot(pf.astype(jnp.bfloat16), nv_ref[:, mine], preferred_element_type=jnp.float32)
        o = (o / total).astype(jnp.bfloat16)
        o_ref[:, at] = jnp.concatenate([o[j * tok : (j + 1) * tok] for j in range(step)], 1)
        return 0

    lax.fori_loop(0, kv * heads // step, one, 0)


def attend(q, keys, values, fk, fv, lengths, seq, kv, hd, step=4):
    tok, wide = q.shape
    rows = keys.shape[1]
    heads = wide // hd // kv
    whole = lambda a: pl.BlockSpec(a.shape, lambda i, l: (0,) * a.ndim)
    kspec = pl.BlockSpec((None, rows, hd), lambda i, l: (seq, 0, 0))
    return pl.pallas_call(
        functools.partial(attend_body, seq=seq, kv=kv, heads=heads, hd=hd, step=step, kb=128),
        out_shape=jax.ShapeDtypeStruct((tok, wide), jnp.bfloat16),
        grid_spec=pltpu.PrefetchScalarGridSpec(num_scalar_prefetch=1, grid=(1,),
            in_specs=[whole(q), kspec, kspec, whole(fk), whole(fv)], out_specs=whole(q),
            scratch_shapes=[pltpu.VMEM((kv, rows // kv, hd), jnp.bfloat16)] * 2),
        compiler_params=pltpu.CompilerParams(vmem_limit_bytes=VMEM),
        cost_estimate=cost(4 * tok * wide * (rows // kv), 4 * rows * hd, tok * wide // hd * (rows // kv)), name="attend")(lengths, q, keys, values, fk, fv)


def project_body(order_ref, w_ref, *refs, nz):
    slots, refs = refs[:nz], refs[nz:]
    pieces, (keep_ref, send_ref, x) = refs[:-3], refs[-3:]
    head, y, g = order_ref[nz], order_ref[nz + 1], order_ref[nz + 2]
    rows, depth = slots[0].shape
    half = rows // 2
    cw = w_ref.shape[1]
    for j in range(nz):
        x[j * rows : (j + 1) * rows] = slots[j][...]

    def put(out, at):
        for j in range(nz):
            low = out[j * rows : j * rows + half]
            high = out[j * rows + half : (j + 1) * rows]
            keep_ref[order_ref[j], :, at] = jnp.where(head == 0, low, high)
            send_ref[order_ref[j], :, at] = jnp.where(head == 0, high, low).astype(jnp.bfloat16)

    at = lambda i: pl.ds(pl.multiple_of(i * cw, cw), cw)
    put(jnp.dot(x[...], w_ref[...], preferred_element_type=jnp.float32), at(y))
    if pieces:
        middle, near, far = pieces
        end = near.shape[0]
        edge = lambda i: pl.ds(pl.multiple_of(i * (depth - end), 128), end)
        out = jnp.dot(x[:, end : depth - end], middle[...], preferred_element_type=jnp.float32)
        out = out + jnp.dot(x[:, edge(g)], near[...], preferred_element_type=jnp.float32)
        out = out + jnp.dot(x[:, edge(1 - g)], far[...], preferred_element_type=jnp.float32)
        put(out, at(1 - y))


def project(slots, w, pieces, order):
    nz = len(slots)
    rows, depth = slots[0].shape
    cols = w.shape[1] * (2 if pieces else 1)
    whole = lambda a: pl.BlockSpec(a.shape, lambda i, o: (0,) * a.ndim)
    shape = (nz, rows // 2, cols)
    return pl.pallas_call(
        functools.partial(project_body, nz=nz),
        out_shape=(jax.ShapeDtypeStruct(shape, jnp.float32), jax.ShapeDtypeStruct(shape, jnp.bfloat16)),
        grid_spec=pltpu.PrefetchScalarGridSpec(
            num_scalar_prefetch=1,
            grid=(1,),
            in_specs=[whole(a) for a in (w, *slots, *pieces)],
            out_specs=[pl.BlockSpec(shape, lambda i, o: (0, 0, 0))] * 2,
            scratch_shapes=[pltpu.VMEM((nz * rows, depth), jnp.bfloat16)],
        ),
        compiler_params=pltpu.CompilerParams(vmem_limit_bytes=VMEM),
        cost_estimate=cost(2 * nz * rows * depth * cols, 2 * (nz * rows * depth + depth * cols)),
        name="project",
    )(order, w, *slots, *pieces)


def expert_body(order_ref, wt_ref, gain_ref, gate_hbm, up_hbm, down_hbm, *refs, nz, eps, show):
    p, refs = refs[:4], refs[4:]
    theirs_ref, ours_ref, refs = refs[0], refs[1], refs[2:]
    if show:
        hid_ref, refs = refs[0], refs[1:]
    wbuf, dbuf, xs, res, act_t, acts, r_t, ss, first_sem, block_sem, down_sem = refs
    head, me = order_ref[nz], order_ref[nz + 3]
    _, part, cw = p[0].shape
    rows = 2 * nz * part
    half = nz // 2
    experts, ff, _ = gate_hbm.shape
    cols = dbuf.shape[3]
    span = lambda c: pl.ds(pl.multiple_of(c * cw, cw), cw)
    sources = (gate_hbm, up_hbm)

    def first(j):
        at = span(order_ref[j])
        return [
            pltpu.make_async_copy(src.at[0, :, at], wbuf.at[0, i, :, at], first_sem.at[i, j])
            for i, src in enumerate(sources)
        ]

    def block(e):
        return [
            pltpu.make_async_copy(src.at[e], wbuf.at[e % 2, i], block_sem.at[i, e % 2])
            for i, src in enumerate(sources)
        ]

    def down_half(i):
        h = 1 - head if i == 0 else head
        at = pl.ds(pl.multiple_of(h * cols, cols), cols)
        return pltpu.make_async_copy(down_hbm.at[:, :, at], dbuf.at[i], down_sem.at[i])

    def start(copies):
        for c in copies:
            c.start()

    def wait(copies):
        for c in copies:
            c.wait()

    for j in range(nz):
        start(first(j))
    if experts > 1:
        start(block(1))
    down_half(0).start()

    def chunk(j, own, other, begin):
        c = order_ref[j]
        at = span(c)
        v = jnp.concatenate([own[...], other[...]], 0).reshape(rows, cw).astype(jnp.float32)
        xs[:, at] = (v * gain_ref[:, at]).astype(jnp.bfloat16)
        wait(first(j))

        def product(i, _):
            out = lax.dot_general(wbuf[0, i, :, at], xs[:, at], LAST, preferred_element_type=jnp.float32)
            res[i] = out if begin else res[i] + out
            return 0

        lax.fori_loop(0, 2, product, 0)
        v = v * v
        total = v[:, :128]
        for i in range(128, cw, 128):
            total = total + v[:, i : i + 128]
        ss[...] = total if begin else ss[...] + total
        if show:

            @pl.when(c // half == head)
            def _():
                to = span(c % half)
                hid_ref[0, :, to] = own[me]
                hid_ref[1, :, to] = other[me]

    chunk(0, p[0], p[2], True)

    def later(j, _):
        chunk(j, p[1].at[j - 1], p[3].at[j - 1], False)
        return 0

    lax.fori_loop(1, nz, later, 0)
    r_t[...] = lax.rsqrt(jnp.sum(ss[...].T, axis=0, keepdims=True) / (nz * cw) + eps)

    def activate(e):
        w = wt_ref[e : e + 1, :] * r_t[...]
        g = res[0] * r_t[...]
        act_t[e * ff : (e + 1) * ff, :] = (g / (1 + jnp.exp(-g)) * (res[1] * w)).astype(jnp.bfloat16)

    activate(0)
    down_half(1).start()
    for e in range(1, experts):
        wait(block(e))

        def product(i, _, e=e):
            res[i] = lax.dot_general(wbuf[e % 2, i], xs[...], LAST, preferred_element_type=jnp.float32)
            return 0

        lax.fori_loop(0, 2, product, 0)
        if e + 1 < experts:
            start(block(e + 1))
        activate(e)
    acts[...] = act_t[...].T
    step = min(1024, cols)
    for i, out in ((0, theirs_ref), (1, ours_ref)):
        down_half(i).wait()

        def columns(n, _, i=i, out=out):
            at = pl.ds(pl.multiple_of(n * step, step), step)
            acc = jnp.dot(acts[...], dbuf[i, :, :, at].reshape(-1, step), preferred_element_type=jnp.float32)
            for k in range(2):
                out[:, k, :, at] = acc[k * nz * part : (k + 1) * nz * part].reshape(nz, part, step).astype(out.dtype)
            return 0

        lax.fori_loop(0, cols // step, columns, 0)


def expert(p, wt, gain, gate_t, up_t, down_w, order, show):
    nz, part, cw = p[0].shape
    experts, ff, depth = gate_t.shape
    rows = 2 * nz * part
    cols = down_w.shape[2] // 2
    out = jax.ShapeDtypeStruct((nz, 2, part, cols), jnp.bfloat16)
    shapes = [out, out]
    if show:
        shapes.append(jax.ShapeDtypeStruct((2, part, nz // 2 * cw), jnp.bfloat16))
    vmem, hbm = pl.BlockSpec(memory_space=pltpu.VMEM), pl.BlockSpec(memory_space=pl.ANY)
    return pl.pallas_call(
        functools.partial(expert_body, nz=nz, eps=1e-5, show=show),
        out_shape=shapes,
        in_specs=[pl.BlockSpec(memory_space=pltpu.SMEM), vmem, vmem, hbm, hbm, hbm] + [vmem] * 4,
        out_specs=[vmem] * len(shapes),
        scratch_shapes=[
            pltpu.VMEM((min(2, experts), 2, ff, depth), jnp.bfloat16),
            pltpu.VMEM((2, experts, ff, cols), jnp.bfloat16),
            pltpu.VMEM((rows, depth), jnp.bfloat16),
            pltpu.VMEM((2, ff, rows), jnp.float32),
            pltpu.VMEM((experts * ff, rows), jnp.bfloat16),
            pltpu.VMEM((rows, experts * ff), jnp.bfloat16),
            pltpu.VMEM((1, rows), jnp.float32),
            pltpu.VMEM((rows, 128), jnp.float32),
            pltpu.SemaphoreType.DMA((2, nz)),
            pltpu.SemaphoreType.DMA((2, 2)),
            pltpu.SemaphoreType.DMA((2,)),
        ],
        compiler_params=pltpu.CompilerParams(vmem_limit_bytes=VMEM),
        cost_estimate=cost(6 * rows * depth * ff * experts, 6 * depth * ff * experts),
        name="expert",
    )(order, wt, gain, gate_t, up_t, down_w, *p)


def settle_body(order_ref, ours_ref, theirs_ref, *refs, nz, adds, spread):
    extra, outs = refs[:adds], refs[adds:]

    def total(zz, i):
        out = ours_ref[zz, i].astype(jnp.float32) + theirs_ref[zz, 1 - i].astype(jnp.float32)
        for ref in extra:
            out = out + ref[zz, i].astype(jnp.float32)
        return out.astype(jnp.bfloat16)

    for j in range(nz):
        zz = lax.rem(order_ref[nz + 3] + j, nz) if spread else j
        for i in range(2):
            if spread:
                outs[j][i] = total(zz, i)
            else:
                outs[0][j, i] = total(zz, i)


def settle(ours, theirs, order, extra, spread, steps=2):
    nz, two, part, cols = ours.shape
    nb = cols // steps
    block = pl.BlockSpec((nz, two, part, nb), lambda i, o: (0, 0, 0, i))
    if spread:
        shapes = [jax.ShapeDtypeStruct((two, part, cols), jnp.bfloat16)] * nz
        specs = [pl.BlockSpec((two, part, nb), lambda i, o: (0, 0, i))] * nz
    else:
        shapes, specs = [jax.ShapeDtypeStruct(ours.shape, jnp.bfloat16)], [block]
    return pl.pallas_call(
        functools.partial(settle_body, nz=nz, adds=len(extra), spread=spread),
        out_shape=shapes,
        grid_spec=pltpu.PrefetchScalarGridSpec(
            num_scalar_prefetch=1, grid=(steps,), in_specs=[block] * (2 + len(extra)), out_specs=specs
        ),
        compiler_params=pltpu.CompilerParams(vmem_limit_bytes=VMEM),
        cost_estimate=cost(4 * ours.size, 2 * ours.size * (3 + len(extra))),
        name="settle",
    )(order, ours, theirs, *extra)


def on_device(
    residual_in, queries, key_cache, value_cache, new_keys, new_values, prefix_len, o_weight,
    norm_gain, expert_ids, route_weights, capacity, gate_w, up_w, down_w, *, nz, ny,
):
    n = nz * ny
    d, head, g = lax.axis_index("dev"), lax.axis_index("head"), lax.axis_index("group")
    z, y = d // ny, d % ny
    tok, q_heads, hd = queries.shape
    seqs = key_cache.shape[0]
    resp = tok // seqs
    part = resp // 2
    f32, bf16 = jnp.float32, jnp.bfloat16

    def shift(x, k):
        pairs = [(a * ny + b, (a + k) % nz * ny + b) for a in range(nz) for b in range(ny)]
        return lax.ppermute(x, "dev", pairs)

    def across(x):
        return lax.ppermute(x, "dev", [(a * ny + b, a * ny + (b + 1) % ny) for a in range(nz) for b in range(ny)])

    partner = lambda x: lax.ppermute(x, "head", [(0, 1), (1, 0)])
    groups = lax.axis_size("group")
    twin = lambda x: lax.ppermute(x, "group", [(i, i ^ 1) for i in range(groups)])

    slot_z = jnp.stack([(z - j) % nz for j in range(nz)])
    order = jnp.concatenate([slot_z, jnp.stack([head, y, g % 2, z])]).astype(jnp.int32)

    w_pieces = ()
    if ny > 1:
        depth = o_weight.shape[0]
        end = depth // 640 * 128
        near = across(lax.dynamic_slice_in_dim(o_weight, g % 2 * (depth - end), end, 0))
        middle = across(o_weight[end : depth - end])
        far = twin(near)
        w_pieces = (middle, near, far)

    width = residual_in.shape[1]
    cw = width // nz
    res = lax.dynamic_index_in_dim(residual_in.reshape(seqs, 2, part, width), head, 1, False)
    columns = lambda zz: lax.dynamic_slice_in_dim(res, zz % nz * cw, cw, 2)

    def line(x):
        forward, back = nz // 2, nz - 1 - nz // 2
        up, down_ = [x], [x]
        for i in range(max(forward, back)):
            if i < forward:
                up.append(shift(up[-1], 1))
            if i < back:
                down_.append(shift(down_[-1], -1))
        return up + down_[:0:-1]

    res_slots = jnp.stack([columns(z)] + [shift(columns(z + k), k) for k in range(1, nz)])
    res_line = jnp.stack([lax.dynamic_index_in_dim(res_slots, (z - a) % nz, 0, False) for a in range(nz)])

    q_flat = queries.reshape(seqs, resp, q_heads * hd)
    flat = lambda x: x.reshape(x.shape[0], -1)
    kv = key_cache.shape[2]
    keys, values = (c.reshape(seqs, -1, hd) for c in (key_cache, value_cache))
    lines = []
    for s in range(seqs):
        rows = slice(s * resp, (s + 1) * resp)
        att = attend(q_flat[s], keys, values, flat(new_keys[rows]), flat(new_values[rows]), prefix_len, s, kv, hd)
        lines.append(line(att))

    packed = jnp.concatenate([expert_ids.astype(f32), route_weights], 1)
    pair = packed[None] if ny == 1 else jnp.stack([packed, across(packed)])
    got = jnp.concatenate([pair] + [shift(pair, k) for k in range(1, nz)], 0)

    slot_dev = jnp.stack([(z - j) % nz * ny + (y + i) % ny for j in range(nz) for i in range(ny)])
    table = jnp.zeros((n, tok, packed.shape[1]), f32).at[slot_dev].set(got).reshape(n * tok, -1)
    top = expert_ids.shape[1]
    ids, weights = table[:, :top].astype(jnp.int32), table[:, top:]
    local = gate_w.shape[0]
    mine = d * local + jnp.arange(local)
    hits = ids[:, :, None] == mine[None, None, :]
    named = jnp.any(hits, 1)
    earlier = jnp.cumsum(named.astype(jnp.int32), 0) - named
    limit = lax.dynamic_slice_in_dim(capacity, d * local, local)
    wt = jnp.where(earlier < limit[None], jnp.sum(jnp.where(hits, weights[:, :, None], 0.0), 1), 0.0)
    wt = wt.reshape(nz, ny, seqs, 2, part, local).transpose(1, 2, 5, 3, 0, 4)
    wt = jnp.where(head == 0, wt, wt[:, :, :, ::-1]).reshape(ny, seqs, local, 2 * nz * part)
    wt = [lax.dynamic_index_in_dim(wt, (y + i) % ny, 0, False) for i in range(ny)]

    gain = norm_gain[None]
    gate_t, up_t = gate_w.swapaxes(1, 2), up_w.swapaxes(1, 2)
    tie = lambda a, b: lax.optimization_barrier((a, b))[0]

    planes = []
    for s in range(seqs):
        keep, send = project(lines[s], o_weight, w_pieces, order)
        if planes:
            keep = tie(keep, planes[-1][0][0])
        projected = (keep + partner(send).astype(f32)).astype(bf16)
        hidden = (res_line[:, s].astype(f32) + projected.astype(f32)).astype(bf16)
        later = jnp.stack([shift(hidden, k) for k in range(1, nz)])
        rows_of = [(hidden, later)]
        if ny > 1:
            head_part = across(hidden)
            rows_of.append((head_part, across(later)))
        pieces = []
        for a, b in rows_of:
            pa = partner(a)
            pieces.append((a, b, pa, partner(b)))
        planes.append(pieces)

    hidden_parts, moe_parts = [None] * seqs, [None] * seqs
    summed = {}

    def run(s, i):
        out = expert(planes[s][i], wt[i][s], gain, gate_t, up_t, down_w, order, show=i == 0)
        if i == 0:
            hidden_parts[s] = out[2]
        summed[s, i] = (out[1], partner(out[0]))

    def other_plane(s):
        ours, theirs = summed[s, 1]
        summed[s, 1] = across((ours.astype(f32) + theirs[:, ::-1].astype(f32)).astype(bf16))

    def finish(s):
        extra = (summed[s, 1],) if ny > 1 else ()
        terms = settle(*summed[s, 0], order, extra, True)
        moved = {}
        for step, count in ((1, nz // 2), (-1, nz - 1 - nz // 2)):
            for i, k in enumerate(range(count, 0, -1)):
                term = terms[step * k]
                if i:
                    term = (term.astype(f32) + moved[step].astype(f32)).astype(bf16)
                moved[step] = shift(term, step)
        final = terms[0].astype(f32)
        for got in moved.values():
            final = final + got.astype(f32)
        moe_parts[s] = final.astype(bf16)

    if ny == 1:
        for s in range(seqs):
            run(s, 0)
            finish(s)
    else:
        for s in range(seqs):
            first_plane = 1 if s and s == seqs - 1 else 0
            run(s, first_plane)
            if first_plane:
                other_plane(s)
            run(s, 1 - first_plane)
            if not first_plane:
                other_plane(s)
            finish(s)
    place = lambda parts: jnp.stack([jnp.where(head == 0, p, p[::-1]) for p in parts]).reshape(tok, -1)
    return place(hidden_parts), place(moe_parts)


def solution(mesh):
    in_specs = (
        P(("group", "dev"), None),
        P(("group", "dev"), "head", None),
        P(("group", "dev"), None, "head", None),
        P(("group", "dev"), None, "head", None),
        P(("group", "dev"), "head", None),
        P(("group", "dev"), "head", None),
        P(("group", "dev")),
        P("head", "dev"),
        P(),
        P(("group", "dev"), None),
        P(("group", "dev"), None),
        P("group"),
        P("dev", None, "head"),
        P("dev", None, "head"),
        P("dev", "head", None),
    )
    out_specs = (P(("group", "dev"), "head"), P(("group", "dev"), "head"))
    n = mesh.shape["dev"]
    spots = [getattr(c, "coords", (0, 0, i)) for i, c in enumerate(mesh.devices[0, :, 0])]
    ny = n // len({p[2] for p in spots})

    def body(*args):
        return on_device(*args, nz=n // ny, ny=ny)

    return jax.shard_map(body, mesh=mesh, in_specs=in_specs, out_specs=out_specs, check_vma=False)
```

```python
import functools

import jax
import jax.numpy as jnp
from jax import lax
from jax.experimental import pallas as pl
from jax.experimental.pallas import tpu as pltpu
from jax.sharding import PartitionSpec as P


VMEM = 58 << 20
LAST = (((1,), (1,)), ((), ()))


def cost(flops, moved, trans=0):
    return pl.CostEstimate(flops=int(flops), bytes_accessed=int(moved), transcendentals=int(trans))


def attend_body(len_ref, q_ref, k_ref, v_ref, nk_ref, nv_ref, o_ref, ks, vs, *, seq, kv, heads, hd, step, kb):
    tok = q_ref.shape[0]
    count = k_ref.shape[0] // kv
    length = len_ref[seq]
    c = hd ** (-0.5) * 1.4426950408889634
    n = kb * kv
    r = lax.broadcasted_iota(jnp.int32, (n, n), 0); cc = lax.broadcasted_iota(jnp.int32, (n, n), 1)
    perm = (cc == (r % kb) * kv + r // kb).astype(jnp.bfloat16)

    def sort(b, _):
        at, to = pl.ds(pl.multiple_of(b * n, n), n), pl.ds(pl.multiple_of(b * kb, kb), kb)
        for src, dst in ((k_ref, ks), (v_ref, vs)):
            t = jnp.dot(perm, src[at], preferred_element_type=jnp.float32).astype(jnp.bfloat16)
            for h in range(kv):
                dst[h, to] = t[h * kb : (h + 1) * kb]
        return 0

    lax.fori_loop(0, count // kb, sort, 0, unroll=2)
    valid = lax.broadcasted_iota(jnp.int32, (1, count), 1) < length
    wide = step * hd
    row = lax.broadcasted_iota(jnp.int32, (step * tok, tok), 0) % tok
    seen = lax.broadcasted_iota(jnp.int32, (step * tok, tok), 1) <= row

    def one(i, _):
        h = i * step // heads
        at = pl.ds(pl.multiple_of(i * wide, wide), wide)
        mine = pl.ds(pl.multiple_of(h * hd, hd), hd)
        q = q_ref[:, at]
        q = jnp.concatenate([q[:, j * hd : (j + 1) * hd] for j in range(step)], 0)
        s = lax.dot_general(q, ks[h], LAST, preferred_element_type=jnp.float32)
        f = lax.dot_general(q, nk_ref[:, mine], LAST, preferred_element_type=jnp.float32)
        s = jnp.where(valid, s, -1e30)
        f = jnp.where(seen, f, -1e30)
        m = jnp.maximum(jnp.max(s, 1, keepdims=True), jnp.max(f, 1, keepdims=True))
        p = jnp.exp2((s - m) * c)
        pf = jnp.exp2((f - m) * c)
        total = jnp.sum(p, 1, keepdims=True) + jnp.sum(pf, 1, keepdims=True)
        o = jnp.dot(p.astype(jnp.bfloat16), vs[h], preferred_element_type=jnp.float32)
        o = o + jnp.dot(pf.astype(jnp.bfloat16), nv_ref[:, mine], preferred_element_type=jnp.float32)
        o = (o / total).astype(jnp.bfloat16)
        o_ref[:, at] = jnp.concatenate([o[j * tok : (j + 1) * tok] for j in range(step)], 1)
        return 0

    lax.fori_loop(0, kv * heads // step, one, 0)


def attend(q, keys, values, fk, fv, lengths, seq, kv, hd, step=4):
    tok, wide = q.shape
    rows = keys.shape[1]
    heads = wide // hd // kv
    whole = lambda a: pl.BlockSpec(a.shape, lambda i, l: (0,) * a.ndim)
    kspec = pl.BlockSpec((None, rows, hd), lambda i, l: (seq, 0, 0))
    return pl.pallas_call(
        functools.partial(attend_body, seq=seq, kv=kv, heads=heads, hd=hd, step=step, kb=128),
        out_shape=jax.ShapeDtypeStruct((tok, wide), jnp.bfloat16),
        grid_spec=pltpu.PrefetchScalarGridSpec(num_scalar_prefetch=1, grid=(1,),
            in_specs=[whole(q), kspec, kspec, whole(fk), whole(fv)], out_specs=whole(q),
            scratch_shapes=[pltpu.VMEM((kv, rows // kv, hd), jnp.bfloat16)] * 2),
        compiler_params=pltpu.CompilerParams(vmem_limit_bytes=VMEM // 2),
        cost_estimate=cost(4 * tok * wide * (rows // kv), 4 * rows * hd, tok * wide // hd * (rows // kv)), name="attend")(lengths, q, keys, values, fk, fv)


def project_body(order_ref, w_ref, *refs, nz):
    slots, refs = refs[:nz], refs[nz:]
    pieces, (keep_ref, send_ref, x) = refs[:-3], refs[-3:]
    head, y, g = order_ref[nz], order_ref[nz + 1], order_ref[nz + 2]
    rows, depth = slots[0].shape
    half = rows // 2
    cw = w_ref.shape[1]
    for j in range(nz):
        x[j * rows : (j + 1) * rows] = slots[j][...]

    def put(out, at):
        for j in range(nz):
            low = out[j * rows : j * rows + half]
            high = out[j * rows + half : (j + 1) * rows]
            keep_ref[order_ref[j], :, at] = jnp.where(head == 0, low, high)
            send_ref[order_ref[j], :, at] = jnp.where(head == 0, high, low).astype(jnp.bfloat16)

    at = lambda i: pl.ds(pl.multiple_of(i * cw, cw), cw)
    put(jnp.dot(x[...], w_ref[...], preferred_element_type=jnp.float32), at(y))
    if pieces:
        middle, near, far = pieces
        end = near.shape[0]
        edge = lambda i: pl.ds(pl.multiple_of(i * (depth - end), 128), end)
        out = jnp.dot(x[:, end : depth - end], middle[...], preferred_element_type=jnp.float32)
        out = out + jnp.dot(x[:, edge(g)], near[...], preferred_element_type=jnp.float32)
        out = out + jnp.dot(x[:, edge(1 - g)], far[...], preferred_element_type=jnp.float32)
        put(out, at(1 - y))


def project(slots, w, pieces, order):
    nz = len(slots)
    rows, depth = slots[0].shape
    cols = w.shape[1] * (2 if pieces else 1)
    whole = lambda a: pl.BlockSpec(a.shape, lambda i, o: (0,) * a.ndim)
    shape = (nz, rows // 2, cols)
    return pl.pallas_call(
        functools.partial(project_body, nz=nz),
        out_shape=(jax.ShapeDtypeStruct(shape, jnp.float32), jax.ShapeDtypeStruct(shape, jnp.bfloat16)),
        grid_spec=pltpu.PrefetchScalarGridSpec(
            num_scalar_prefetch=1,
            grid=(1,),
            in_specs=[whole(a) for a in (w, *slots, *pieces)],
            out_specs=[pl.BlockSpec(shape, lambda i, o: (0, 0, 0))] * 2,
            scratch_shapes=[pltpu.VMEM((nz * rows, depth), jnp.bfloat16)],
        ),
        compiler_params=pltpu.CompilerParams(vmem_limit_bytes=VMEM * 2 // 3),
        cost_estimate=cost(2 * nz * rows * depth * cols, 2 * (nz * rows * depth + depth * cols)),
        name="project",
    )(order, w, *slots, *pieces)


def expert_body(order_ref, wt_ref, gain_ref, gate_hbm, up_hbm, down_hbm, *refs, nz, eps, show):
    p, refs = refs[:4], refs[4:]
    theirs_ref, ours_ref, refs = refs[0], refs[1], refs[2:]
    if show:
        hid_ref, refs = refs[0], refs[1:]
    pbuf, wbuf, dbuf, xs, res, act_t, acts, r_t, ss, row_sem, first_sem, block_sem, down_sem = refs
    head, me = order_ref[nz], order_ref[nz + 3]
    part, cw = pbuf.shape[3:]
    rows = 2 * nz * part
    half = nz // 2
    experts, ff, _ = gate_hbm.shape
    cols = dbuf.shape[3]
    span = lambda c: pl.ds(pl.multiple_of(c * cw, cw), cw)
    sources = (gate_hbm, up_hbm)

    def gathered(j):
        both = (p[0], p[2]) if isinstance(j, int) and j == 0 else (p[1].at[j - 1], p[3].at[j - 1])
        return [pltpu.make_async_copy(src, pbuf.at[j, k], row_sem.at[k, j]) for k, src in enumerate(both)]

    def first(j):
        at = span(order_ref[j])
        return [
            pltpu.make_async_copy(src.at[0, :, at], wbuf.at[0, i, :, at], first_sem.at[i, j])
            for i, src in enumerate(sources)
        ]

    def block(e):
        return [
            pltpu.make_async_copy(src.at[e], wbuf.at[e % 2, i], block_sem.at[i, e % 2])
            for i, src in enumerate(sources)
        ]

    def down_half(i):
        h = 1 - head if i == 0 else head
        at = pl.ds(pl.multiple_of(h * cols, cols), cols)
        return pltpu.make_async_copy(down_hbm.at[:, :, at], dbuf.at[i], down_sem.at[i])

    def start(copies):
        for c in copies:
            c.start()

    def wait(copies):
        for c in copies:
            c.wait()

    for j in range(nz):
        start(gathered(j))
        start(first(j))
    if experts > 1:
        start(block(1))
    down_half(0).start()

    def chunk(j, _):
        c = order_ref[j]
        at = span(c)
        for k in range(2):
            pltpu.make_async_copy(p[0], pbuf.at[j, k], row_sem.at[k, j]).wait()
        v = pbuf[j].reshape(rows, cw).astype(jnp.float32)
        x = (v * gain_ref[:, at]).astype(jnp.bfloat16)
        xs[:, at] = x
        wait(first(j))
        for i in range(2):
            out = lax.dot_general(wbuf[0, i, :, at], x, LAST, preferred_element_type=jnp.float32)
            res[i] = jnp.where(j > 0, res[i], 0.0) + out
        v = v * v
        total = v[:, :128]
        for i in range(128, cw, 128):
            total = total + v[:, i : i + 128]
        ss[...] = jnp.where(j > 0, ss[...], 0.0) + total
        if show:

            @pl.when(c // half == head)
            def _():
                to = span(c % half)
                hid_ref[head, :, to] = pbuf[j, 0, me]
                hid_ref[1 - head, :, to] = pbuf[j, 1, me]

        return 0

    lax.fori_loop(0, nz, chunk, 0)
    r_t[...] = lax.rsqrt(jnp.sum(ss[...].T, axis=0, keepdims=True) / (nz * cw) + eps)

    def activate(e):
        w = wt_ref[e : e + 1, :] * r_t[...]
        g = res[0] * r_t[...]
        act_t[e * ff : (e + 1) * ff, :] = (g / (1 + jnp.exp(-g)) * (res[1] * w)).astype(jnp.bfloat16)

    activate(0)
    down_half(1).start()
    for e in range(1, experts):
        wait(block(e))

        for i in range(2):
            res[i] = lax.dot_general(wbuf[e % 2, i], xs[...], LAST, preferred_element_type=jnp.float32)
        if e + 1 < experts:
            start(block(e + 1))
        activate(e)
    acts[...] = act_t[...].T
    step = min(1024, cols)
    for i, out in ((0, theirs_ref), (1, ours_ref)):
        down_half(i).wait()

        def columns(n, _, i=i, out=out):
            at = pl.ds(pl.multiple_of(n * step, step), step)
            acc = jnp.dot(acts[...], dbuf[i, :, :, at].reshape(-1, step), preferred_element_type=jnp.float32)
            for k in range(2):
                out[:, k, :, at] = acc[k * nz * part : (k + 1) * nz * part].reshape(nz, part, step).astype(out.dtype)
            return 0

        lax.fori_loop(0, cols // step, columns, 0)


def expert(p, wt, gain, gate_t, up_t, down_w, order, show):
    nz, part, cw = p[0].shape
    experts, ff, depth = gate_t.shape
    rows = 2 * nz * part
    cols = down_w.shape[2] // 2
    out = jax.ShapeDtypeStruct((nz, 2, part, cols), jnp.bfloat16)
    shapes = [out, out]
    if show:
        shapes.append(jax.ShapeDtypeStruct((2, part, nz // 2 * cw), jnp.bfloat16))
    held = 4 * depth * ff * (2 * min(2, experts)) // 2 + 4 * experts * ff * cols + 4 * rows * depth + 8 * ff * rows
    held += 4 * experts * ff * rows + 4 * rows * cols
    vmem, hbm = pl.BlockSpec(memory_space=pltpu.VMEM), pl.BlockSpec(memory_space=pltpu.HBM)
    return pl.pallas_call(
        functools.partial(expert_body, nz=nz, eps=1e-5, show=show),
        out_shape=shapes,
        in_specs=[pl.BlockSpec(memory_space=pltpu.SMEM), vmem, vmem, hbm, hbm, hbm] + [hbm] * 4,
        out_specs=[vmem] * len(shapes),
        scratch_shapes=[
            pltpu.VMEM((nz, 2, nz, part, cw), jnp.bfloat16),
            pltpu.VMEM((min(2, experts), 2, ff, depth), jnp.bfloat16),
            pltpu.VMEM((2, experts, ff, cols), jnp.bfloat16),
            pltpu.VMEM((rows, depth), jnp.bfloat16),
            pltpu.VMEM((2, ff, rows), jnp.float32),
            pltpu.VMEM((experts * ff, rows), jnp.bfloat16),
            pltpu.VMEM((rows, experts * ff), jnp.bfloat16),
            pltpu.VMEM((1, rows), jnp.float32),
            pltpu.VMEM((rows, 128), jnp.float32),
            pltpu.SemaphoreType.DMA((2, nz)),
            pltpu.SemaphoreType.DMA((2, nz)),
            pltpu.SemaphoreType.DMA((2, 2)),
            pltpu.SemaphoreType.DMA((2,)),
        ],
        compiler_params=pltpu.CompilerParams(vmem_limit_bytes=min(VMEM, held + (8 << 20))),
        cost_estimate=cost(6 * rows * depth * ff * experts, 6 * depth * ff * experts),
        name="expert",
    )(order, wt, gain, gate_t, up_t, down_w, *p)


def settle_body(order_ref, ours_ref, theirs_ref, *refs, nz, adds, spread):
    extra, outs = refs[:adds], refs[adds:]

    def total(zz, i):
        out = ours_ref[zz, i].astype(jnp.float32) + theirs_ref[zz, 1 - i].astype(jnp.float32)
        for ref in extra:
            out = out + ref[zz, i].astype(jnp.float32)
        return out.astype(jnp.bfloat16)

    for j in range(nz):
        zz = lax.rem(order_ref[nz + 3] + j, nz) if spread else j
        for i in range(2):
            if spread:
                outs[j][i] = total(zz, i)
            else:
                outs[0][j, i] = total(zz, i)


def settle(ours, theirs, order, extra, spread, steps=2):
    nz, two, part, cols = ours.shape
    nb = cols // steps
    block = pl.BlockSpec((nz, two, part, nb), lambda i, o: (0, 0, 0, i))
    if spread:
        shapes = [jax.ShapeDtypeStruct((two, part, cols), jnp.bfloat16)] * nz
        specs = [pl.BlockSpec((two, part, nb), lambda i, o: (0, 0, i))] * nz
    else:
        shapes, specs = [jax.ShapeDtypeStruct(ours.shape, jnp.bfloat16)], [block]
    return pl.pallas_call(
        functools.partial(settle_body, nz=nz, adds=len(extra), spread=spread),
        out_shape=shapes,
        grid_spec=pltpu.PrefetchScalarGridSpec(
            num_scalar_prefetch=1, grid=(steps,), in_specs=[block] * (2 + len(extra)), out_specs=specs
        ),
        compiler_params=pltpu.CompilerParams(vmem_limit_bytes=VMEM // 2),
        cost_estimate=cost(4 * ours.size, 2 * ours.size * (3 + len(extra))),
        name="settle",
    )(order, ours, theirs, *extra)


def on_device(
    residual_in, queries, key_cache, value_cache, new_keys, new_values, prefix_len, o_weight,
    norm_gain, expert_ids, route_weights, capacity, gate_w, up_w, down_w, *, nz, ny,
):
    n = nz * ny
    d, head, g = lax.axis_index("dev"), lax.axis_index("head"), lax.axis_index("group")
    z, y = d // ny, d % ny
    tok, q_heads, hd = queries.shape
    seqs = key_cache.shape[0]
    resp = tok // seqs
    part = resp // 2
    f32, bf16 = jnp.float32, jnp.bfloat16

    def shift(x, k):
        pairs = [(a * ny + b, (a + k) % nz * ny + b) for a in range(nz) for b in range(ny)]
        return lax.ppermute(x, "dev", pairs)

    def across(x):
        return lax.ppermute(x, "dev", [(a * ny + b, a * ny + (b + 1) % ny) for a in range(nz) for b in range(ny)])

    partner = lambda x: lax.ppermute(x, "head", [(0, 1), (1, 0)])
    groups = lax.axis_size("group")
    twin = lambda x: lax.ppermute(x, "group", [(i, i ^ 1) for i in range(groups)])

    slot_z = jnp.stack([(z - j) % nz for j in range(nz)])
    order = jnp.concatenate([slot_z, jnp.stack([head, y, g % 2, z])]).astype(jnp.int32)

    w_pieces = ()
    if ny > 1:
        depth = o_weight.shape[0]
        end = depth // 640 * 128
        near = across(lax.dynamic_slice_in_dim(o_weight, g % 2 * (depth - end), end, 0))
        middle = across(o_weight[end : depth - end])
        far = twin(near)
        w_pieces = (middle, near, far)

    width = residual_in.shape[1]
    cw = width // nz
    res = lax.dynamic_index_in_dim(residual_in.reshape(seqs, 2, part, width), head, 1, False)
    columns = lambda zz: lax.dynamic_slice_in_dim(res, zz % nz * cw, cw, 2)

    def line(x):
        forward, back = nz // 2, nz - 1 - nz // 2
        up, down_ = [x], [x]
        for i in range(max(forward, back)):
            if i < forward:
                up.append(shift(up[-1], 1))
            if i < back:
                down_.append(shift(down_[-1], -1))
        return up + down_[:0:-1]

    res_slots = jnp.stack([columns(z)] + [shift(columns(z + k), k) for k in range(1, nz)])
    res_line = jnp.stack([lax.dynamic_index_in_dim(res_slots, (z - a) % nz, 0, False) for a in range(nz)])

    q_flat = queries.reshape(seqs, resp, q_heads * hd)
    flat = lambda x: x.reshape(x.shape[0], -1)
    kv = key_cache.shape[2]
    keys, values = (c.reshape(seqs, -1, hd) for c in (key_cache, value_cache))
    lines = []
    for s in range(seqs):
        rows = slice(s * resp, (s + 1) * resp)
        att = attend(q_flat[s], keys, values, flat(new_keys[rows]), flat(new_values[rows]), prefix_len, s, kv, hd)
        lines.append(line(att))

    packed = jnp.concatenate([expert_ids.astype(f32), route_weights], 1)
    pair = packed[None] if ny == 1 else jnp.stack([packed, across(packed)])
    got = jnp.concatenate([pair] + [shift(pair, k) for k in range(1, nz)], 0)

    slot_dev = jnp.stack([(z - j) % nz * ny + (y + i) % ny for j in range(nz) for i in range(ny)])
    table = jnp.zeros((n, tok, packed.shape[1]), f32).at[slot_dev].set(got).reshape(n * tok, -1)
    top = expert_ids.shape[1]
    ids, weights = table[:, :top].astype(jnp.int32), table[:, top:]
    local = gate_w.shape[0]
    mine = d * local + jnp.arange(local)
    hits = ids[:, :, None] == mine[None, None, :]
    named = jnp.any(hits, 1)
    earlier = jnp.cumsum(named.astype(jnp.int32), 0) - named
    limit = lax.dynamic_slice_in_dim(capacity, d * local, local)
    wt = jnp.where(earlier < limit[None], jnp.sum(jnp.where(hits, weights[:, :, None], 0.0), 1), 0.0)
    wt = wt.reshape(nz, ny, seqs, 2, part, local).transpose(1, 2, 5, 3, 0, 4)
    wt = jnp.where(head == 0, wt, wt[:, :, :, ::-1]).reshape(ny, seqs, local, 2 * nz * part)
    wt = [lax.dynamic_index_in_dim(wt, (y + i) % ny, 0, False) for i in range(ny)]

    gain = norm_gain[None]
    gate_t, up_t = gate_w.swapaxes(1, 2), up_w.swapaxes(1, 2)
    tie = lambda a, b: lax.optimization_barrier((a, b))[0]

    planes = []
    for s in range(seqs):
        keep, send = project(lines[s], o_weight, w_pieces, order)
        if planes:
            keep = tie(keep, planes[-1][0][0])
        projected = (keep + partner(send).astype(f32)).astype(bf16)
        hidden = (res_line[:, s].astype(f32) + projected.astype(f32)).astype(bf16)
        later = jnp.stack([shift(hidden, k) for k in range(1, nz)])
        rows_of = [(hidden, later)]
        if ny > 1:
            head_part = across(hidden)
            rows_of.append((head_part, across(later)))
        pieces = []
        for a, b in rows_of:
            pa = partner(a)
            pieces.append((a, b, pa, partner(b)))
        planes.append(pieces)

    hidden_parts, moe_parts = [None] * seqs, [None] * seqs
    summed = {}

    def run(s, i):
        out = expert(planes[s][i], wt[i][s], gain, gate_t, up_t, down_w, order, show=i == 0)
        if i == 0:
            hidden_parts[s] = out[2]
        summed[s, i] = (out[1], partner(out[0]))

    def other_plane(s):
        ours, theirs = summed[s, 1]
        summed[s, 1] = across((ours.astype(f32) + theirs[:, ::-1].astype(f32)).astype(bf16))

    def finish(s):
        extra = (summed[s, 1],) if ny > 1 else ()
        terms = settle(*summed[s, 0], order, extra, True)
        got = []
        if s < seqs - 1:
            for k in range(1, nz):
                got.append(shift(terms[k], k))
        else:
            for step, count in ((1, nz // 2), (-1, nz - 1 - nz // 2)):
                moved = None
                for i, k in enumerate(range(count, 0, -1)):
                    term = terms[step * k]
                    if i:
                        term = (term.astype(f32) + moved.astype(f32)).astype(bf16)
                    moved = shift(term, step)
                got.append(moved)
        final = terms[0].astype(f32)
        for term in got:
            final = final + term.astype(f32)
        final = final.astype(bf16)
        moe_parts[s] = jnp.where(head == 0, final, final[::-1])

    if ny == 1:
        for s in range(seqs):
            run(s, 0)
            finish(s)
    else:
        for s in range(seqs):
            first_plane = 1 if s and s == seqs - 1 else 0
            run(s, first_plane)
            if first_plane:
                other_plane(s)
            run(s, 1 - first_plane)
            if not first_plane:
                other_plane(s)
            finish(s)
    place = lambda parts: jnp.concatenate([p.reshape(resp, -1) for p in parts])
    hidden_out = place(hidden_parts)
    moe_out = place(moe_parts)
    return hidden_out, moe_out


def solution(mesh):
    in_specs = (
        P(("group", "dev"), None),
        P(("group", "dev"), "head", None),
        P(("group", "dev"), None, "head", None),
        P(("group", "dev"), None, "head", None),
        P(("group", "dev"), "head", None),
        P(("group", "dev"), "head", None),
        P(("group", "dev")),
        P("head", "dev"),
        P(),
        P(("group", "dev"), None),
        P(("group", "dev"), None),
        P("group"),
        P("dev", None, "head"),
        P("dev", None, "head"),
        P("dev", "head", None),
    )
    out_specs = (P(("group", "dev"), "head"), P(("group", "dev"), "head"))
    n = mesh.shape["dev"]
    spots = [getattr(c, "coords", (0, 0, i)) for i, c in enumerate(mesh.devices[0, :, 0])]
    ny = n // len({p[2] for p in spots})

    def body(*args):
        return on_device(*args, nz=n // ny, ny=ny)

    return jax.shard_map(body, mesh=mesh, in_specs=in_specs, out_specs=out_specs, check_vma=False)
```

```python
import functools

import jax
import jax.numpy as jnp
from jax import lax
from jax.experimental import pallas as pl
from jax.experimental.pallas import tpu as pltpu
from jax.sharding import PartitionSpec as P


VMEM = 58 << 20
LAST = (((1,), (1,)), ((), ()))


def cost(flops, moved, trans=0):
    return pl.CostEstimate(flops=int(flops), bytes_accessed=int(moved), transcendentals=int(trans))


def attend_body(len_ref, q_ref, k_ref, v_ref, nk_ref, nv_ref, o_ref, ks, vs, *, seq, kv, heads, hd, step, kb):
    tok = q_ref.shape[0]
    count = k_ref.shape[0] // kv
    length = len_ref[seq]
    c = hd ** (-0.5) * 1.4426950408889634
    n = kb * kv
    r = lax.broadcasted_iota(jnp.int32, (n, n), 0); cc = lax.broadcasted_iota(jnp.int32, (n, n), 1)
    perm = (cc == (r % kb) * kv + r // kb).astype(jnp.bfloat16)

    def sort(b, _):
        at, to = pl.ds(pl.multiple_of(b * n, n), n), pl.ds(pl.multiple_of(b * kb, kb), kb)
        for src, dst in ((k_ref, ks), (v_ref, vs)):
            t = jnp.dot(perm, src[at], preferred_element_type=jnp.float32).astype(jnp.bfloat16)
            for h in range(kv):
                dst[h, to] = t[h * kb : (h + 1) * kb]
        return 0

    lax.fori_loop(0, count // kb, sort, 0, unroll=2)
    valid = lax.broadcasted_iota(jnp.int32, (1, count), 1) < length
    wide = step * hd
    row = lax.broadcasted_iota(jnp.int32, (step * tok, tok), 0) % tok
    seen = lax.broadcasted_iota(jnp.int32, (step * tok, tok), 1) <= row

    def one(i, _):
        h = i * step // heads
        at = pl.ds(pl.multiple_of(i * wide, wide), wide)
        mine = pl.ds(pl.multiple_of(h * hd, hd), hd)
        q = q_ref[:, at]
        q = jnp.concatenate([q[:, j * hd : (j + 1) * hd] for j in range(step)], 0)
        s = lax.dot_general(q, ks[h], LAST, preferred_element_type=jnp.float32)
        f = lax.dot_general(q, nk_ref[:, mine], LAST, preferred_element_type=jnp.float32)
        s = jnp.where(valid, s, -1e30)
        f = jnp.where(seen, f, -1e30)
        m = jnp.maximum(jnp.max(s, 1, keepdims=True), jnp.max(f, 1, keepdims=True))
        p = jnp.exp2((s - m) * c)
        pf = jnp.exp2((f - m) * c)
        total = jnp.sum(p, 1, keepdims=True) + jnp.sum(pf, 1, keepdims=True)
        o = jnp.dot(p.astype(jnp.bfloat16), vs[h], preferred_element_type=jnp.float32)
        o = o + jnp.dot(pf.astype(jnp.bfloat16), nv_ref[:, mine], preferred_element_type=jnp.float32)
        o = (o / total).astype(jnp.bfloat16)
        o_ref[:, at] = jnp.concatenate([o[j * tok : (j + 1) * tok] for j in range(step)], 1)
        return 0

    lax.fori_loop(0, kv * heads // step, one, 0)


def attend(q, keys, values, fk, fv, lengths, seq, kv, hd, step=4):
    tok, wide = q.shape
    rows = keys.shape[1]
    heads = wide // hd // kv
    whole = lambda a: pl.BlockSpec(a.shape, lambda i, l: (0,) * a.ndim)
    kspec = pl.BlockSpec((None, rows, hd), lambda i, l: (seq, 0, 0))
    return pl.pallas_call(
        functools.partial(attend_body, seq=seq, kv=kv, heads=heads, hd=hd, step=step, kb=128),
        out_shape=jax.ShapeDtypeStruct((tok, wide), jnp.bfloat16),
        grid_spec=pltpu.PrefetchScalarGridSpec(num_scalar_prefetch=1, grid=(1,),
            in_specs=[whole(q), kspec, kspec, whole(fk), whole(fv)], out_specs=whole(q),
            scratch_shapes=[pltpu.VMEM((kv, rows // kv, hd), jnp.bfloat16)] * 2),
        compiler_params=pltpu.CompilerParams(vmem_limit_bytes=VMEM * 2 // 5),
        cost_estimate=cost(4 * tok * wide * (rows // kv), 4 * rows * hd, tok * wide // hd * (rows // kv)), name="attend")(lengths, q, keys, values, fk, fv)


def project_body(order_ref, w_ref, *refs, nz):
    slots, refs = refs[:nz], refs[nz:]
    pieces, (keep_ref, send_ref, x) = refs[:-3], refs[-3:]
    head, y, g = order_ref[nz], order_ref[nz + 1], order_ref[nz + 2]
    rows, depth = slots[0].shape
    half = rows // 2
    cw = w_ref.shape[1]
    for j in range(nz):
        x[j * rows : (j + 1) * rows] = slots[j][...]

    def put(out, at):
        for j in range(nz):
            low = out[j * rows : j * rows + half]
            high = out[j * rows + half : (j + 1) * rows]
            keep_ref[order_ref[j], :, at] = jnp.where(head == 0, low, high)
            send_ref[order_ref[j], :, at] = jnp.where(head == 0, high, low).astype(jnp.bfloat16)

    at = lambda i: pl.ds(pl.multiple_of(i * cw, cw), cw)
    put(jnp.dot(x[...], w_ref[...], preferred_element_type=jnp.float32), at(y))
    if pieces:
        middle, near, far = pieces
        end = near.shape[0]
        edge = lambda i: pl.ds(pl.multiple_of(i * (depth - end), 128), end)
        out = jnp.dot(x[:, end : depth - end], middle[...], preferred_element_type=jnp.float32)
        out = out + jnp.dot(x[:, edge(g)], near[...], preferred_element_type=jnp.float32)
        out = out + jnp.dot(x[:, edge(1 - g)], far[...], preferred_element_type=jnp.float32)
        put(out, at(1 - y))


def project(slots, w, pieces, order):
    nz = len(slots)
    rows, depth = slots[0].shape
    cols = w.shape[1] * (2 if pieces else 1)
    whole = lambda a: pl.BlockSpec(a.shape, lambda i, o: (0,) * a.ndim)
    shape = (nz, rows // 2, cols)
    return pl.pallas_call(
        functools.partial(project_body, nz=nz),
        out_shape=(jax.ShapeDtypeStruct(shape, jnp.float32), jax.ShapeDtypeStruct(shape, jnp.bfloat16)),
        grid_spec=pltpu.PrefetchScalarGridSpec(
            num_scalar_prefetch=1,
            grid=(1,),
            in_specs=[whole(a) for a in (w, *slots, *pieces)],
            out_specs=[pl.BlockSpec(shape, lambda i, o: (0, 0, 0))] * 2,
            scratch_shapes=[pltpu.VMEM((nz * rows, depth), jnp.bfloat16)],
        ),
        compiler_params=pltpu.CompilerParams(vmem_limit_bytes=VMEM * 2 // 3),
        cost_estimate=cost(2 * nz * rows * depth * cols, 2 * (nz * rows * depth + depth * cols)),
        name="project",
    )(order, w, *slots, *pieces)


def expert_body(order_ref, wt_ref, gain_ref, gate_hbm, up_hbm, down_hbm, *refs, nz, eps, show):
    p, refs = refs[:4], refs[4:]
    theirs_ref, ours_ref, refs = refs[0], refs[1], refs[2:]
    if show:
        hid_ref, refs = refs[0], refs[1:]
    pbuf, wbuf, dbuf, xs, res, act_t, acts, r_t, ss, row_sem, first_sem, block_sem, down_sem = refs
    head, me = order_ref[nz], order_ref[nz + 3]
    part, cw = pbuf.shape[3:]
    rows = 2 * nz * part
    half = nz // 2
    experts, ff, _ = gate_hbm.shape
    cols = dbuf.shape[3]
    span = lambda c: pl.ds(pl.multiple_of(c * cw, cw), cw)
    sources = (gate_hbm, up_hbm)

    def gathered(j):
        both = (p[0], p[2]) if isinstance(j, int) and j == 0 else (p[1].at[j - 1], p[3].at[j - 1])
        return [pltpu.make_async_copy(src, pbuf.at[j, k], row_sem.at[k, j]) for k, src in enumerate(both)]

    def first(j):
        at = span(order_ref[j])
        return [
            pltpu.make_async_copy(src.at[0, :, at], wbuf.at[0, i, :, at], first_sem.at[i, j])
            for i, src in enumerate(sources)
        ]

    def block(e):
        return [
            pltpu.make_async_copy(src.at[e], wbuf.at[e % 2, i], block_sem.at[i, e % 2])
            for i, src in enumerate(sources)
        ]

    def down_half(i):
        h = 1 - head if i == 0 else head
        at = pl.ds(pl.multiple_of(h * cols, cols), cols)
        return pltpu.make_async_copy(down_hbm.at[:, :, at], dbuf.at[i], down_sem.at[i])

    def start(copies):
        for c in copies:
            c.start()

    def wait(copies):
        for c in copies:
            c.wait()

    for j in range(nz):
        start(gathered(j))
        start(first(j))
    if experts > 1:
        start(block(1))
    down_half(0).start()

    def chunk(j, _):
        c = order_ref[j]
        at = span(c)
        for k in range(2):
            pltpu.make_async_copy(p[0], pbuf.at[j, k], row_sem.at[k, j]).wait()
        v = pbuf[j].reshape(rows, cw).astype(jnp.float32)
        x = (v * gain_ref[:, at]).astype(jnp.bfloat16)
        xs[:, at] = x
        wait(first(j))
        for i in range(2):
            out = lax.dot_general(wbuf[0, i, :, at], x, LAST, preferred_element_type=jnp.float32)
            res[i] = jnp.where(j > 0, res[i], 0.0) + out
        v = v * v
        total = v[:, :128]
        for i in range(128, cw, 128):
            total = total + v[:, i : i + 128]
        ss[...] = jnp.where(j > 0, ss[...], 0.0) + total
        if show:

            @pl.when(c // half == head)
            def _():
                to = span(c % half)
                hid_ref[head, :, to] = pbuf[j, 0, me]
                hid_ref[1 - head, :, to] = pbuf[j, 1, me]

        return 0

    lax.fori_loop(0, nz, chunk, 0)
    r_t[...] = lax.rsqrt(jnp.sum(ss[...].T, axis=0, keepdims=True) / (nz * cw) + eps)

    def activate(e):
        w = wt_ref[e : e + 1, :] * r_t[...]
        g = res[0] * r_t[...]
        act_t[e * ff : (e + 1) * ff, :] = (g / (1 + jnp.exp(-g)) * (res[1] * w)).astype(jnp.bfloat16)

    activate(0)
    down_half(1).start()
    for e in range(1, experts):
        wait(block(e))

        for i in range(2):
            res[i] = lax.dot_general(wbuf[e % 2, i], xs[...], LAST, preferred_element_type=jnp.float32)
        if e + 1 < experts:
            start(block(e + 1))
        activate(e)
    acts[...] = act_t[...].T
    step = min(1024, cols)
    for i, out in ((0, theirs_ref), (1, ours_ref)):
        down_half(i).wait()

        def columns(n, _, i=i, out=out):
            at = pl.ds(pl.multiple_of(n * step, step), step)
            acc = jnp.dot(acts[...], dbuf[i, :, :, at].reshape(-1, step), preferred_element_type=jnp.float32)
            for k in range(2):
                out[:, k, :, at] = acc[k * nz * part : (k + 1) * nz * part].reshape(nz, part, step).astype(out.dtype)
            return 0

        lax.fori_loop(0, cols // step, columns, 0)


def expert(p, wt, gain, gate_t, up_t, down_w, order, show):
    nz, part, cw = p[0].shape
    experts, ff, depth = gate_t.shape
    rows = 2 * nz * part
    cols = down_w.shape[2] // 2
    out = jax.ShapeDtypeStruct((nz, 2, part, cols), jnp.bfloat16)
    shapes = [out, out]
    if show:
        shapes.append(jax.ShapeDtypeStruct((2, part, nz // 2 * cw), jnp.bfloat16))
    held = 4 * depth * ff * (2 * min(2, experts)) // 2 + 4 * experts * ff * cols + 4 * rows * depth + 8 * ff * rows
    held += 4 * experts * ff * rows + 4 * rows * cols
    vmem, hbm = pl.BlockSpec(memory_space=pltpu.VMEM), pl.BlockSpec(memory_space=pltpu.HBM)
    return pl.pallas_call(
        functools.partial(expert_body, nz=nz, eps=1e-5, show=show),
        out_shape=shapes,
        in_specs=[pl.BlockSpec(memory_space=pltpu.SMEM), vmem, vmem, hbm, hbm, hbm] + [hbm] * 4,
        out_specs=[vmem] * len(shapes),
        scratch_shapes=[
            pltpu.VMEM((nz, 2, nz, part, cw), jnp.bfloat16),
            pltpu.VMEM((min(2, experts), 2, ff, depth), jnp.bfloat16),
            pltpu.VMEM((2, experts, ff, cols), jnp.bfloat16),
            pltpu.VMEM((rows, depth), jnp.bfloat16),
            pltpu.VMEM((2, ff, rows), jnp.float32),
            pltpu.VMEM((experts * ff, rows), jnp.bfloat16),
            pltpu.VMEM((rows, experts * ff), jnp.bfloat16),
            pltpu.VMEM((1, rows), jnp.float32),
            pltpu.VMEM((rows, 128), jnp.float32),
            pltpu.SemaphoreType.DMA((2, nz)),
            pltpu.SemaphoreType.DMA((2, nz)),
            pltpu.SemaphoreType.DMA((2, 2)),
            pltpu.SemaphoreType.DMA((2,)),
        ],
        compiler_params=pltpu.CompilerParams(vmem_limit_bytes=min(VMEM, held + (5 << 20))),
        cost_estimate=cost(6 * rows * depth * ff * experts, 6 * depth * ff * experts),
        name="expert",
    )(order, wt, gain, gate_t, up_t, down_w, *p)


def settle_body(order_ref, ours_ref, theirs_ref, *refs, nz, adds, spread):
    extra, outs = refs[:adds], refs[adds:]

    def total(zz, i):
        out = ours_ref[zz, i].astype(jnp.float32) + theirs_ref[zz, 1 - i].astype(jnp.float32)
        for ref in extra:
            out = out + ref[zz, i].astype(jnp.float32)
        return out.astype(jnp.bfloat16)

    for j in range(nz):
        zz = lax.rem(order_ref[nz + 3] + j, nz) if spread else j
        for i in range(2):
            if spread:
                outs[j][i] = total(zz, i)
            else:
                outs[0][j, i] = total(zz, i)


def settle(ours, theirs, order, extra, spread, steps=2):
    nz, two, part, cols = ours.shape
    nb = cols // steps
    block = pl.BlockSpec((nz, two, part, nb), lambda i, o: (0, 0, 0, i))
    if spread:
        shapes = [jax.ShapeDtypeStruct((two, part, cols), jnp.bfloat16)] * nz
        specs = [pl.BlockSpec((two, part, nb), lambda i, o: (0, 0, i))] * nz
    else:
        shapes, specs = [jax.ShapeDtypeStruct(ours.shape, jnp.bfloat16)], [block]
    return pl.pallas_call(
        functools.partial(settle_body, nz=nz, adds=len(extra), spread=spread),
        out_shape=shapes,
        grid_spec=pltpu.PrefetchScalarGridSpec(
            num_scalar_prefetch=1, grid=(steps,), in_specs=[block] * (2 + len(extra)), out_specs=specs
        ),
        compiler_params=pltpu.CompilerParams(vmem_limit_bytes=min(VMEM // 2, 16 * ours.size + (4 << 20))),
        cost_estimate=cost(4 * ours.size, 2 * ours.size * (3 + len(extra))),
        name="settle",
    )(order, ours, theirs, *extra)


def on_device(
    residual_in, queries, key_cache, value_cache, new_keys, new_values, prefix_len, o_weight,
    norm_gain, expert_ids, route_weights, capacity, gate_w, up_w, down_w, *, nz, ny,
):
    n = nz * ny
    d, head, g = lax.axis_index("dev"), lax.axis_index("head"), lax.axis_index("group")
    z, y = d // ny, d % ny
    tok, q_heads, hd = queries.shape
    seqs = key_cache.shape[0]
    resp = tok // seqs
    part = resp // 2
    f32, bf16 = jnp.float32, jnp.bfloat16

    def shift(x, k):
        pairs = [(a * ny + b, (a + k) % nz * ny + b) for a in range(nz) for b in range(ny)]
        return lax.ppermute(x, "dev", pairs)

    def across(x):
        return lax.ppermute(x, "dev", [(a * ny + b, a * ny + (b + 1) % ny) for a in range(nz) for b in range(ny)])

    partner = lambda x: lax.ppermute(x, "head", [(0, 1), (1, 0)])
    groups = lax.axis_size("group")
    twin = lambda x: lax.ppermute(x, "group", [(i, i ^ 1) for i in range(groups)])

    slot_z = jnp.stack([(z - j) % nz for j in range(nz)])
    order = jnp.concatenate([slot_z, jnp.stack([head, y, g % 2, z])]).astype(jnp.int32)

    w_pieces = ()
    if ny > 1:
        depth = o_weight.shape[0]
        end = depth // 640 * 128
        near = across(lax.dynamic_slice_in_dim(o_weight, g % 2 * (depth - end), end, 0))
        middle = across(o_weight[end : depth - end])
        far = twin(near)
        w_pieces = (middle, near, far)

    width = residual_in.shape[1]
    cw = width // nz
    res = lax.dynamic_index_in_dim(residual_in.reshape(seqs, 2, part, width), head, 1, False)
    columns = lambda zz: lax.dynamic_slice_in_dim(res, zz % nz * cw, cw, 2)

    def line(x):
        forward, back = nz // 2, nz - 1 - nz // 2
        up, down_ = [x], [x]
        for i in range(max(forward, back)):
            if i < forward:
                up.append(shift(up[-1], 1))
            if i < back:
                down_.append(shift(down_[-1], -1))
        return up + down_[:0:-1]

    res_slots = jnp.stack([columns(z)] + [shift(columns(z + k), k) for k in range(1, nz)])
    res_line = jnp.stack([lax.dynamic_index_in_dim(res_slots, (z - a) % nz, 0, False) for a in range(nz)])

    q_flat = queries.reshape(seqs, resp, q_heads * hd)
    flat = lambda x: x.reshape(x.shape[0], -1)
    kv = key_cache.shape[2]
    keys, values = (c.reshape(seqs, -1, hd) for c in (key_cache, value_cache))
    lines = []
    for s in range(seqs):
        rows = slice(s * resp, (s + 1) * resp)
        att = attend(q_flat[s], keys, values, flat(new_keys[rows]), flat(new_values[rows]), prefix_len, s, kv, hd)
        lines.append(line(att))

    packed = jnp.concatenate([expert_ids.astype(f32), route_weights], 1)
    pair = packed[None] if ny == 1 else jnp.stack([packed, across(packed)])
    got = jnp.concatenate([pair] + [shift(pair, k) for k in range(1, nz)], 0)

    slot_dev = jnp.stack([(z - j) % nz * ny + (y + i) % ny for j in range(nz) for i in range(ny)])
    table = jnp.zeros((n, tok, packed.shape[1]), f32).at[slot_dev].set(got).reshape(n * tok, -1)
    top = expert_ids.shape[1]
    ids, weights = table[:, :top].astype(jnp.int32), table[:, top:]
    local = gate_w.shape[0]
    mine = d * local + jnp.arange(local)
    hits = ids[:, :, None] == mine[None, None, :]
    named = jnp.any(hits, 1)
    earlier = jnp.cumsum(named.astype(jnp.int32), 0) - named
    limit = lax.dynamic_slice_in_dim(capacity, d * local, local)
    wt = jnp.where(earlier < limit[None], jnp.sum(jnp.where(hits, weights[:, :, None], 0.0), 1), 0.0)
    wt = wt.reshape(nz, ny, seqs, 2, part, local).transpose(1, 2, 5, 3, 0, 4)
    wt = jnp.where(head == 0, wt, wt[:, :, :, ::-1]).reshape(ny, seqs, local, 2 * nz * part)
    wt = [lax.dynamic_index_in_dim(wt, (y + i) % ny, 0, False) for i in range(ny)]

    gain = norm_gain[None]
    gate_t, up_t = gate_w.swapaxes(1, 2), up_w.swapaxes(1, 2)
    tie = lambda a, b: lax.optimization_barrier((a, b))[0]

    planes = []
    for s in range(seqs):
        keep, send = project(lines[s], o_weight, w_pieces, order)
        if planes:
            keep = tie(keep, planes[-1][0][0])
        projected = (keep + partner(send).astype(f32)).astype(bf16)
        hidden = (res_line[:, s].astype(f32) + projected.astype(f32)).astype(bf16)
        later = jnp.stack([shift(hidden, k) for k in range(1, nz)])
        rows_of = [(hidden, later)]
        if ny > 1:
            head_part = across(hidden)
            rows_of.append((head_part, across(later)))
        pieces = []
        for a, b in rows_of:
            pa = partner(a)
            pieces.append((a, b, pa, partner(b)))
        planes.append(pieces)

    hidden_parts, moe_parts = [None] * seqs, [None] * seqs
    summed = {}

    def run(s, i):
        out = expert(planes[s][i], wt[i][s], gain, gate_t, up_t, down_w, order, show=i == 0)
        if i == 0:
            hidden_parts[s] = out[2]
        summed[s, i] = (out[1], partner(out[0]))

    def other_plane(s):
        ours, theirs = summed[s, 1]
        summed[s, 1] = across((ours.astype(f32) + theirs[:, ::-1].astype(f32)).astype(bf16))

    def finish(s):
        extra = (summed[s, 1],) if ny > 1 else ()
        terms = settle(*summed[s, 0], order, extra, True)
        got = []
        if s < seqs - 1:
            for k in range(1, nz):
                got.append(shift(terms[k], k))
        else:
            for step, count in ((1, nz // 2), (-1, nz - 1 - nz // 2)):
                moved = None
                for i, k in enumerate(range(count, 0, -1)):
                    term = terms[step * k]
                    if i:
                        term = (term.astype(f32) + moved.astype(f32)).astype(bf16)
                    moved = shift(term, step)
                got.append(moved)
        final = terms[0].astype(f32)
        for term in got:
            final = final + term.astype(f32)
        final = final.astype(bf16)
        moe_parts[s] = jnp.where(head == 0, final, final[::-1])

    if ny == 1:
        for s in range(seqs):
            run(s, 0)
            finish(s)
    else:
        for s in range(seqs):
            first_plane = 1 if s and s == seqs - 1 else 0
            run(s, first_plane)
            if first_plane:
                other_plane(s)
            run(s, 1 - first_plane)
            if not first_plane:
                other_plane(s)
            finish(s)
    place = lambda parts: jnp.concatenate([p.reshape(resp, -1) for p in parts])
    hidden_out = place(hidden_parts)
    moe_out = place(moe_parts)
    return hidden_out, moe_out


def solution(mesh):
    in_specs = (
        P(("group", "dev"), None),
        P(("group", "dev"), "head", None),
        P(("group", "dev"), None, "head", None),
        P(("group", "dev"), None, "head", None),
        P(("group", "dev"), "head", None),
        P(("group", "dev"), "head", None),
        P(("group", "dev")),
        P("head", "dev"),
        P(),
        P(("group", "dev"), None),
        P(("group", "dev"), None),
        P("group"),
        P("dev", None, "head"),
        P("dev", None, "head"),
        P("dev", "head", None),
    )
    out_specs = (P(("group", "dev"), "head"), P(("group", "dev"), "head"))
    n = mesh.shape["dev"]
    spots = [getattr(c, "coords", (0, 0, i)) for i, c in enumerate(mesh.devices[0, :, 0])]
    ny = n // len({p[2] for p in spots})

    def body(*args):
        return on_device(*args, nz=n // ny, ny=ny)

    return jax.shard_map(body, mesh=mesh, in_specs=in_specs, out_specs=out_specs, check_vma=False)
```
